256 devices in a mesh: section: 4 (over x), space: 64 (over z, y, core).
Axes of the slice: x: 4, y: 4, z: 8, core: 2. Of those that a mesh axis runs over, the one named last changes fastest.
Arguments:
- encoder_inputs: bfloat16 [4, 1, 128, 256, 2, 64], P('section', None, None, 'space'), may hold values from -6 to 6
- upper_inputs: bfloat16 [4, 1, 128, 256, 2, 64], P('section', None, None, 'space'), may hold values from -6 to 6
- output_cotangent: bfloat16 [1, 128, 256, 2, 64], P(None, None, 'space'), may hold values from -6 to 6
- weights: bfloat16 [4, 4, 3, 128, 1152], P('section'), may hold values from -0.15625 to 0.15625
- biases: float32 [4, 4, 128], P('section'), may hold values from -3 to 3
Outputs:
- encoder_grad: bfloat16 [4, 1, 128, 256, 2, 64], P('section', None, None, 'space')
- upper_grad: bfloat16 [4, 1, 128, 256, 2, 64], P('section', None, None, 'space')
- weight_grad: float32 [4, 4, 3, 128, 1152], P('section')
- bias_grad: float32 [4, 4, 128], P('section')
The draws below stay inside these ranges and needn't reach their ends.
All inputs are finite; a program needn't handle non-finite values.
Results may differ from the reference program's by a relative error of at most 0.018.
Values may be sent and summed in bfloat16 or wider, within the bound.
No kernel may reach another device: no remote copies, remote signals or barrier semaphores. Data moves between devices by JAX's collectives and lax.ppermute only.
A program may use at most 64 MiB of HBM per device.

```python
import jax
import jax.numpy as jnp
from jax import lax

C = 128
YC = 2
ZC = 64
MICRO = 1
CONVS = 4
SECTIONS = 4
X = 256


def level_of(rng, extent, pieces, least, largest):
    factor_of, own = 1.0, jax.random.fold_in(rng, 6)
    for position, shards_of in pieces:
        draws = jnp.exp(jax.random.uniform(jax.random.fold_in(own, position), (shards_of,), jnp.float32, least / len(pieces), largest / len(pieces)))
        factor_of = factor_of * jnp.repeat(draws, extent[position] // shards_of).reshape([-1 if axis == position else 1 for axis in range(len(extent))])
    return factor_of


def normal_values(key, dims, deviation, limit, pieces=(), held_as=jnp.bfloat16):
    drawn = jax.random.normal(key, dims, jnp.float32) * deviation
    if len(pieces) > 0:
        drawn = level_of(key, dims, pieces, -0.22, 0.18) * drawn
    return jnp.clip(drawn, min=-limit, max=limit).astype(held_as)


def setup_inputs(seed: int = 0) -> dict:
    key_of = jax.random.split(jax.random.key(seed), 6)
    encoder_inputs = normal_values(key_of[0], (SECTIONS, MICRO, C, X, YC, ZC), 1.0, 6.0, ((0, 4), (3, 64)))
    upper_inputs = normal_values(key_of[1], (SECTIONS, MICRO, C, X, YC, ZC), 1.0, 6.0, ((0, 4), (3, 64)))
    output_cotangent = normal_values(key_of[2], (MICRO, C, X, YC, ZC), 1.0, 6.0, ((2, 64),))
    weights = normal_values(key_of[3], (SECTIONS, CONVS, 3, C, 9 * C), (27 * C // 2) ** -0.5, 0.15625, ((0, 4),))
    biases = normal_values(key_of[4], (SECTIONS, CONVS, C), 0.5, 3.0, ((0, 4),), jnp.float32)
    return dict(encoder_inputs=encoder_inputs, upper_inputs=upper_inputs, output_cotangent=output_cotangent, weights=weights, biases=biases)


def rounded(value):
    return lax.optimization_barrier(value.astype(jnp.bfloat16))

def to_kernel(weight):
    width = weight.shape[1]
    return weight.astype(jnp.float32).reshape(3, width, 3, 3, width).transpose(1, 4, 0, 2, 3)

def from_kernel(kernel):
    width = kernel.shape[0]
    return kernel.transpose(2, 0, 3, 4, 1).reshape(3, width, 9 * width)

def convolve(field, kernel):
    return lax.conv_general_dilated(field[None], kernel, (1, 1, 1), [(1, 1), (1, 1), (1, 1)], dimension_numbers=('NCDHW', 'OIDHW', 'NCDHW'), precision=lax.Precision.HIGHEST)[0]

def silu_slope(pre):
    logistic = jax.nn.sigmoid(pre)
    return logistic * (1.0 + pre * (1.0 - logistic))

def block_forward(inputs, first_kernel, second_kernel, first_bias, second_bias):
    first_pre = convolve(inputs.astype(jnp.float32), first_kernel) + first_bias[:, None, None, None]
    first_act = rounded(jax.nn.silu(first_pre))
    second_pre = convolve(first_act.astype(jnp.float32), second_kernel) + second_bias[:, None, None, None]
    return (first_pre, first_act, second_pre)

def block_backward(inputs, first_pre, first_act, second_pre, first_kernel, second_kernel, cotangent):
    second_grad = rounded(cotangent.astype(jnp.float32) * silu_slope(second_pre))
    outputs, pullback = jax.vjp(convolve, first_act.astype(jnp.float32), second_kernel)
    hidden_grad, second_kernel_grad = pullback(second_grad.astype(jnp.float32))
    first_grad = rounded(hidden_grad * silu_slope(first_pre))
    outputs, pullback = jax.vjp(convolve, inputs.astype(jnp.float32), first_kernel)
    input_grad, first_kernel_grad = pullback(first_grad.astype(jnp.float32))
    weight_terms = jnp.stack([from_kernel(first_kernel_grad), from_kernel(second_kernel_grad)])
    bias_terms = jnp.stack([lax.optimization_barrier(jnp.sum(first_grad.astype(jnp.float32), axis=(1, 2, 3))), lax.optimization_barrier(jnp.sum(second_grad.astype(jnp.float32), axis=(1, 2, 3)))])
    return (rounded(input_grad), weight_terms, bias_terms)

def reference(encoder_inputs, upper_inputs, output_cotangent, weights, biases):
    kernels = [[to_kernel(weights[section, layer]) for layer in range(CONVS)] for section in range(SECTIONS)]
    weight_grad = jnp.zeros(weights.shape, jnp.float32)
    bias_grad = jnp.zeros(biases.shape, jnp.float32)
    encoder_list = [[None] * MICRO for section in range(SECTIONS)]
    upper_list = [[None] * MICRO for section in range(SECTIONS)]
    for micro in range(MICRO):
        saved_encoder = []
        saved_decoder = []
        for section in range(SECTIONS):
            inputs = encoder_inputs[section, micro]
            encoded = block_forward(inputs, kernels[section][0], kernels[section][1], biases[section, 0], biases[section, 1])
            encoder_out = rounded(jax.nn.silu(encoded[2]))
            decoder_input = rounded(encoder_out.astype(jnp.float32) + upper_inputs[section, micro].astype(jnp.float32))
            decoded = block_forward(decoder_input, kernels[section][2], kernels[section][3], biases[section, 2], biases[section, 3])
            saved_encoder.append((inputs, encoded[0], encoded[1], encoded[2]))
            saved_decoder.append((decoder_input, decoded[0], decoded[1], decoded[2]))
        cotangent = output_cotangent[micro]
        for section in range(SECTIONS):
            saved = saved_decoder[section]
            input_grad, weight_terms, bias_terms = block_backward(saved[0], saved[1], saved[2], saved[3], kernels[section][2], kernels[section][3], cotangent)
            upper_list[section][micro] = input_grad
            weight_grad = weight_grad.at[section, 2:4].add(weight_terms)
            bias_grad = bias_grad.at[section, 2:4].add(bias_terms)
            cotangent = input_grad
        above = jnp.zeros(output_cotangent.shape[1:], jnp.bfloat16)
        for section in range(SECTIONS - 1, -1, -1):
            cotangent = rounded(upper_list[section][micro].astype(jnp.float32) + above.astype(jnp.float32))
            saved = saved_encoder[section]
            input_grad, weight_terms, bias_terms = block_backward(saved[0], saved[1], saved[2], saved[3], kernels[section][0], kernels[section][1], cotangent)
            encoder_list[section][micro] = input_grad
            weight_grad = weight_grad.at[section, 0:2].add(weight_terms)
            bias_grad = bias_grad.at[section, 0:2].add(bias_terms)
            above = input_grad
    encoder_grad = jnp.stack([jnp.stack(encoder_list[section]) for section in range(SECTIONS)])
    upper_grad = jnp.stack([jnp.stack(upper_list[section]) for section in range(SECTIONS)])
    return (encoder_grad, upper_grad, weight_grad, bias_grad)
```

```python
import jax
import jax.numpy as jnp
from jax import lax
from jax.experimental import pallas as pl
from jax.experimental.pallas import tpu as pltpu
from jax.sharding import PartitionSpec as P

C = 128
Y = 2
Z = 64
W = Y * C
SPACE = 64
SECTIONS = 4
ROWS = 4
CELLS = ROWS * Z
BF = jnp.bfloat16
F32 = jnp.float32
VMEM = pl.BlockSpec(memory_space=pltpu.VMEM)
SMEM = pl.BlockSpec(memory_space=pltpu.SMEM)


def z_shifts(value):
    count = value.shape[0]
    wide = value.astype(F32)
    depth = lax.broadcasted_iota(jnp.int32, (count, W), 0) % Z
    below = jnp.where(depth == 0, 0.0, pltpu.roll(wide, 1, 0)).astype(BF)
    above = jnp.where(depth == Z - 1, 0.0, pltpu.roll(wide, count - 1, 0)).astype(BF)
    return below, value, above


def tap(w, a, b, c):
    lane = (3 * b + c) * C
    return w[a, :, lane : lane + C]


def row_mask(count, first, place):
    row = lax.broadcasted_iota(jnp.int32, (count * Z, W), 0) // Z + (first + ROWS * place)
    return (row >= 0) & (row < SPACE * ROWS)


def conv(value, w, out_rows):
    stacked = jnp.concatenate(z_shifts(value), axis=1)
    total = None
    for a in range(3):
        kernel = jnp.concatenate(
            [
                jnp.concatenate([tap(w, a, y_in - y_out + 1, c) for c in range(3) for y_in in range(Y)], axis=1)
                for y_out in range(Y)
            ],
            axis=0,
        )
        part = lax.dot_general(
            stacked[a * Z : (a + out_rows) * Z],
            kernel,
            (((1,), (1,)), ((), ())),
            preferred_element_type=F32,
        )
        total = part if total is None else total + part
    return total


def conv_adjoint(value, w, out_rows):
    below, same, above = z_shifts(value)
    stacked = jnp.concatenate([above, same, below], axis=1)
    total = None
    for a in range(3):
        kernel = jnp.concatenate(
            [
                jnp.concatenate([tap(w, a, y_in - y_out + 1, c) for y_in in range(Y)], axis=1)
                for c in range(3)
                for y_out in range(Y)
            ],
            axis=0,
        )
        part = lax.dot_general(
            stacked[(2 - a) * Z : (2 - a + out_rows) * Z],
            kernel,
            (((1,), (0,)), ((), ())),
            preferred_element_type=F32,
        )
        total = part if total is None else total + part
    return total


def forward_kernel(
    place_ref, w_ref, bias_ref, far_left, left, own, right, far_right, *outs
):
    place = place_ref[0]
    own_enc = own[0:CELLS]
    inputs = jnp.concatenate(
        [far_left[...], left[0:CELLS], own_enc, right[0:CELLS], far_right[...]], axis=0
    )
    upper = jnp.concatenate(
        [left[CELLS : 2 * CELLS], own[CELLS : 2 * CELLS], right[CELLS : 2 * CELLS]], axis=0
    )
    enc_v, enc_h, dec_v, dec_h, enc_s1, enc_s2, dec_s1, dec_s2 = outs

    def bias(layer):
        return bias_ref[layer : layer + 1, :]

    def middle(value, halo, keep):
        return value[(halo - keep) * Z : (halo + ROWS + keep) * Z]

    def gate(pre):
        logistic = jax.nn.sigmoid(pre)
        return pre * logistic, logistic, pre

    def slope(pre, logistic):
        return logistic * (1.0 + pre * (1.0 - logistic))

    enc_v[...] = middle(inputs, 6, 1)
    pre = conv(inputs, w_ref.at[0], 14) + bias(0)
    act, logistic, _ = gate(pre)
    enc_s1[...] = middle(slope(pre, logistic), 5, 1)
    act = jnp.where(row_mask(14, -5, place), act, 0.0).astype(BF)
    enc_h[...] = middle(act, 5, 1)
    pre = conv(act, w_ref.at[1], 12) + bias(1)
    act, logistic, _ = gate(pre)
    enc_s2[...] = middle(slope(pre, logistic), 4, 2)
    act = act.astype(BF).astype(F32) + upper.astype(F32)
    act = jnp.where(row_mask(12, -4, place), act, 0.0).astype(BF)
    dec_v[...] = middle(act, 4, 1)
    pre = conv(act, w_ref.at[2], 10) + bias(2)
    act, logistic, _ = gate(pre)
    dec_s1[...] = middle(slope(pre, logistic), 3, 1)
    act = jnp.where(row_mask(10, -3, place), act, 0.0).astype(BF)
    dec_h[...] = middle(act, 3, 1)
    pre = conv(act, w_ref.at[3], 8) + bias(3)
    act, logistic, _ = gate(pre)
    dec_s2[...] = middle(slope(pre, logistic), 2, 2)


def sds(rows, dtype):
    return jax.ShapeDtypeStruct((rows * Z, W), dtype)


def forward(place, weights, biases, far_left, left, own, right, far_right):
    return pl.pallas_call(
        forward_kernel,
        out_shape=[sds(6, BF)] * 4 + [sds(6, F32), sds(8, F32), sds(6, F32), sds(8, F32)],
        in_specs=[SMEM] + [VMEM] * 7,
        out_specs=[VMEM] * 8,
        compiler_params=pltpu.CompilerParams(vmem_limit_bytes=40 << 20),
        cost_estimate=pl.CostEstimate(flops=6 * 10**9, bytes_accessed=8 << 20, transcendentals=0),
        name="forward",
    )(place, weights, biases, far_left, left, own, right, far_right)


def tick_kernel(layer, turn, seeded, place_ref, w_ref, *refs):
    names = list(refs)
    s1_ref, s2_ref = names[0:2]
    cots = [names[2:5]]
    rest = names[5:]
    if seeded == "sum":
        cots.append(rest[0:3])
        rest = rest[3:]
    outs = rest[-5:]
    place = place_ref[0]

    def run():
        def window(three):
            low, mid, high = (ref[...] for ref in three)
            return jnp.concatenate([low, mid, high], axis=0)

        g = window(cots[0]).astype(F32)
        if len(cots) > 1:
            g = (g + window(cots[1]).astype(F32)).astype(BF).astype(F32)
        second = (g * s2_ref[...]).astype(BF)
        outs[0][...] = second[2 * Z : 2 * Z + CELLS]
        first = conv_adjoint(second, w_ref.at[layer + 1], 6) * s1_ref[...]
        first = jnp.where(row_mask(6, -1, place), first, 0.0).astype(BF)
        outs[1][...] = first[Z : Z + CELLS]
        grad = conv_adjoint(first, w_ref.at[layer], 4).astype(BF)
        outs[2][...] = grad
        outs[3][...] = grad[0 : 2 * Z]
        outs[4][...] = grad[CELLS - 2 * Z : CELLS]

    if turn is None:
        run()
        return

    def carry():
        for out, ref in zip(outs, rest[:5]):
            out[...] = ref[...]

    mine = place_ref[1] == turn
    pl.when(mine)(run)
    pl.when(jnp.logical_not(mine))(carry)


def tick(layer, turn, place, weights, slopes, cot, skip=None, state=None):
    args = [place, weights, *slopes, *cot]
    seeded = "plain"
    if skip is not None:
        args += list(skip)
        seeded = "sum"
    if state is not None:
        args += list(state)
    return pl.pallas_call(
        lambda *refs: tick_kernel(layer, turn, seeded, *refs),
        out_shape=[sds(4, BF)] * 3 + [sds(2, BF)] * 2,
        in_specs=[SMEM] + [VMEM] * (len(args) - 1),
        out_specs=[VMEM] * 5,
        compiler_params=pltpu.CompilerParams(vmem_limit_bytes=24 << 20),
        cost_estimate=pl.CostEstimate(flops=3 * 10**9, bytes_accessed=4 << 20, transcendentals=0),
        name="tick",
    )(*args)


PARTS = 4
PIECES = 8
USED = 27 * C // PARTS
PIECE = 112
PART = PIECES * PIECE
GRID_AXES = ("section", "space")


def shifted(source_section, by, step):
    pairs = []
    for place in range(SPACE):
        if 0 <= place + step < SPACE:
            source = source_section * SPACE + place
            pairs.append((source, source + by * SPACE + step))
    return pairs


def hand_on(state, source_section, by):
    grad, low, high = state[2:5]
    middle = lax.ppermute(grad, GRID_AXES, shifted(source_section, by, 0))
    before = lax.ppermute(high, GRID_AXES, shifted(source_section, by, 1))
    after = lax.ppermute(low, GRID_AXES, shifted(source_section, by, -1))
    return (before, middle, after)


def beside(array, step):
    pairs = [(place, place + step) for place in range(SPACE) if 0 <= place + step < SPACE]
    return lax.ppermute(array, "space", pairs)


def weight_kernel(place_ref, u1_ref, v1_ref, u2_ref, v2_ref, keep_ref, send_ref, held):
    core = place_ref[0] % 2
    for layer, (u_ref, v_ref) in enumerate(((u1_ref, v1_ref), (u2_ref, v2_ref))):
        grads = u_ref[...]
        wide = grads.astype(F32)
        turned = wide.T.astype(BF)
        stacked = jnp.concatenate(z_shifts(v_ref[...]), axis=1)
        for a in range(3):
            product = jnp.dot(
                turned, stacked[a * Z : a * Z + CELLS], preferred_element_type=F32
            )

            def block(y_out, c, y_in):
                lane = (c * Y + y_in) * C
                return product[y_out * C : (y_out + 1) * C, lane : lane + C]

            for c in range(3):
                blocks = (block(1, c, 0), block(0, c, 0) + block(1, c, 1), block(0, c, 1))
                for b in range(3):
                    value = blocks[b].astype(BF)
                    row = (9 * a + 3 * b + c) * (C // PARTS)
                    for part in range(PARTS):
                        held[layer, part, row : row + C // PARTS, :] = value[
                            part * (C // PARTS) : (part + 1) * (C // PARTS)
                        ]
        sums = jnp.sum(wide, axis=0, keepdims=True)
        sums = sums[:, 0:C] + sums[:, C : 2 * C]
        for part in range(PARTS):
            held[layer, part, USED:PART, :] = jnp.broadcast_to(sums, (PART - USED, C)).astype(BF)
    keep_ref[...] = held[core]
    send_ref[...] = held[1 - core]


def weight_terms(place, u1, v1, u2, v2):
    shape = jax.ShapeDtypeStruct((PARTS, PART, C), BF)
    return pl.pallas_call(
        weight_kernel,
        out_shape=[shape, shape],
        in_specs=[SMEM] + [VMEM] * 4,
        out_specs=[VMEM] * 2,
        scratch_shapes=[pltpu.VMEM((2, PARTS, PART, C), BF)],
        compiler_params=pltpu.CompilerParams(vmem_limit_bytes=24 << 20),
        cost_estimate=pl.CostEstimate(flops=2 * 10**9, bytes_accessed=4 << 20, transcendentals=0),
        name="weights",
    )(place, u1, v1, u2, v2)


def split_kernel(ways, spot, place_ref, own_ref, *refs):
    count = len(refs) - 1 - ways
    arrived, outs, total = refs[:count], refs[count:-1], refs[-1]
    value = own_ref[...].astype(F32)
    for ref in arrived:
        value = value + ref[...].astype(F32)
    here = spot(place_ref[0])
    total[...] = value.reshape(total.shape)
    outs[0][...] = total[here]
    for step in range(1, ways):
        outs[step][...] = total[(here + step) % ways].astype(BF)


def split(place, own, arrived, ways, spot):
    rows = own.shape[-2] * (own.shape[0] if own.ndim == 3 else 1) // ways
    return pl.pallas_call(
        lambda *refs: split_kernel(ways, spot, *refs),
        out_shape=[jax.ShapeDtypeStruct((rows, C), F32)]
        + [jax.ShapeDtypeStruct((rows, C), BF)] * (ways - 1),
        in_specs=[SMEM] + [VMEM] * (1 + len(arrived)),
        out_specs=[VMEM] * ways,
        scratch_shapes=[pltpu.VMEM((ways, rows, C), F32)],
        compiler_params=pltpu.CompilerParams(vmem_limit_bytes=16 << 20),
        name="split",
    )(place, own, *arrived)


def join_kernel(ways, spot, place_ref, *refs):
    here = spot(place_ref[0])
    out = refs[-1]
    for step in range(ways):
        out[(here - step + ways) % ways] = refs[step][...]


def join(place, pieces, spot):
    ways = len(pieces)
    rows = pieces[0].shape[0]
    joined = pl.pallas_call(
        lambda *refs: join_kernel(ways, spot, *refs),
        out_shape=jax.ShapeDtypeStruct((ways, rows, C), BF),
        in_specs=[SMEM] + [VMEM] * ways,
        out_specs=VMEM,
        compiler_params=pltpu.CompilerParams(vmem_limit_bytes=16 << 20),
        name="join",
    )(place, *pieces)
    return joined.reshape(ways * rows, C)


def last_kernel(own_ref, arrived_ref, out_ref):
    out_ref[...] = (own_ref[...] + arrived_ref[...].astype(F32)).astype(BF)


def core_of(place):
    return place % 2


def y_of(place):
    return (place // 2) % 4


def z_high(place):
    return place // 16


def z_low(place):
    return (place // 8) % 2


def core_step(place, step):
    return place ^ 1


def y_step(place, step):
    return (place // 8) * 8 + ((place // 2 + step) % 4) * 2 + place % 2


def z_high_step(place, step):
    return (place + 16 * step) % SPACE


def z_low_step(place, step):
    return place ^ 8


def send(array, move, step):
    return lax.ppermute(array, "space", [(place, move(place, step)) for place in range(SPACE)])


def scatter_sum(place, keep, given):
    arrived = [send(given, core_step, 1)]
    pieces = split(place, keep, arrived, 4, y_of)
    arrived = [send(pieces[step], y_step, step) for step in range(1, 4)]
    pieces = split(place, pieces[0], arrived, 4, z_high)
    arrived = [send(pieces[step], z_high_step, step) for step in range(1, 4)]
    pieces = split(place, pieces[0], arrived, 2, z_low)
    arrived = send(pieces[1], z_low_step, 1)
    return pl.pallas_call(
        last_kernel,
        out_shape=jax.ShapeDtypeStruct((PIECE, C), BF),
        in_specs=[VMEM] * 2,
        out_specs=VMEM,
        name="last",
    )(pieces[0], arrived)


def gather_parts(place, piece):
    whole = join(place, [piece, send(piece, z_low_step, 1)], z_low)
    whole = join(place, [whole] + [send(whole, z_high_step, step) for step in range(1, 4)], z_high)
    whole = join(place, [whole] + [send(whole, y_step, step) for step in range(1, 4)], y_of)
    return whole, send(whole, core_step, 1)


def unpack_kernel(place_ref, mine_ref, other_ref, *refs):
    weight_ref, bias_ref = refs[-2:]
    layer = pl.program_id(0)

    def write(ref):
        for part in range(PARTS):
            rows = slice(part * (C // PARTS), (part + 1) * (C // PARTS))
            for a in range(3):
                for j in range(9):
                    row = part * PART + (9 * a + j) * (C // PARTS)
                    weight_ref[0, a, rows, j * C : (j + 1) * C] = ref[
                        row : row + C // PARTS, :
                    ].astype(F32)
        bias_ref[0] = ref[USED : USED + 16, :].astype(F32)[0:1]

    mine = layer == place_ref[0] % 2
    pl.when(mine)(lambda: write(mine_ref))
    pl.when(jnp.logical_not(mine))(lambda: write(other_ref))


def unpack(place, mine, other, first, onto):
    shapes = [
        jax.ShapeDtypeStruct((4, 3, C, 9 * C), F32),
        jax.ShapeDtypeStruct((4, 1, C), F32),
    ]
    args = [place, mine, other]
    specs = [SMEM, VMEM, VMEM]
    aliases = {}
    if onto is not None:
        args += list(onto)
        specs += [pl.BlockSpec(memory_space=pl.ANY)] * 2
        aliases = {3: 0, 4: 1}
    return pl.pallas_call(
        unpack_kernel,
        grid=(2,),
        out_shape=shapes,
        in_specs=specs,
        out_specs=[
            pl.BlockSpec((1, 3, C, 9 * C), lambda layer: (first + layer, 0, 0, 0)),
            pl.BlockSpec((1, 1, C), lambda layer: (first + layer, 0, 0)),
        ],
        input_output_aliases=aliases,
        compiler_params=pltpu.CompilerParams(vmem_limit_bytes=24 << 20),
        name="unpack",
    )(*args)


def to_cells(block):
    return block.transpose(1, 3, 2, 0).reshape(CELLS, W)


def from_cells(field):
    return field.reshape(ROWS, Z, Y, C).transpose(3, 0, 2, 1)[None, None]


def on_device(encoder_inputs, upper_inputs, output_cotangent, weights, biases):
    section = lax.axis_index("section")
    space = lax.axis_index("space")
    place = jnp.stack([space, section]).astype(jnp.int32)
    kernels = weights[0]
    bias_rows = jnp.concatenate([biases[0], biases[0]], axis=1)
    enc = to_cells(encoder_inputs[0, 0])
    own = jnp.concatenate(
        [enc, to_cells(upper_inputs[0, 0]), to_cells(output_cotangent[0])], axis=0
    )
    left = beside(own, 1)
    right = beside(own, -1)
    far_left = beside(enc[CELLS - 2 * Z :], 2)
    far_right = beside(enc[: 2 * Z], -2)
    enc_v, enc_h, dec_v, dec_h, enc_s1, enc_s2, dec_s1, dec_s2 = forward(
        place, kernels, bias_rows, far_left, left, own, right, far_right
    )
    cot = (left[3 * CELLS - 2 * Z :], own[2 * CELLS :], right[2 * CELLS : 2 * CELLS + 2 * Z])
    slopes = (dec_s1, dec_s2)
    state = tick(2, None, place, kernels, slopes, cot)
    for turn in range(1, SECTIONS):
        cot = hand_on(state, turn - 1, 1)
        state = tick(2, turn, place, kernels, slopes, cot, state=state)
    upper = state
    skip = (beside(upper[4], 1), upper[2], beside(upper[3], -1))
    slopes = (enc_s1, enc_s2)
    state = tick(0, None, place, kernels, slopes, skip)
    dec_keep, dec_given = weight_terms(place, upper[1], dec_v, upper[0], dec_h)
    dec_piece = scatter_sum(place, dec_keep, dec_given)
    for turn in range(SECTIONS - 2, -1, -1):
        cot = hand_on(state, turn + 1, -1)
        state = tick(0, turn, place, kernels, slopes, cot, skip=skip, state=state)
    enc_keep, enc_given = weight_terms(place, state[1], enc_v, state[0], enc_h)
    enc_piece = scatter_sum(place, enc_keep, enc_given)
    totals = unpack(place, *gather_parts(place, dec_piece), 2, None)
    weight_total, bias_total = unpack(place, *gather_parts(place, enc_piece), 0, totals)
    return (
        from_cells(state[2]),
        from_cells(upper[2]),
        weight_total[None],
        bias_total.reshape(1, 4, C),
    )


def solution(mesh):
    return jax.shard_map(
        on_device,
        mesh=mesh,
        in_specs=(
            P("section", None, None, "space", None, None),
            P("section", None, None, "space", None, None),
            P(None, None, "space", None, None),
            P("section", None, None, None, None),
            P("section", None, None),
        ),
        out_specs=(
            P("section", None, None, "space", None, None),
            P("section", None, None, "space", None, None),
            P("section", None, None, None, None),
            P("section", None, None),
        ),
        check_vma=False,
    )
```

```python
import jax
import jax.numpy as jnp
from jax import lax
from jax.experimental import pallas as pl
from jax.experimental.pallas import tpu as pltpu
from jax.sharding import PartitionSpec as P


C = 128
Y = 2
Z = 64
W = Y * C
SPACE = 64
SECTIONS = 4
ROWS = 4
CELLS = ROWS * Z
BF = jnp.bfloat16
F32 = jnp.float32
VMEM = pl.BlockSpec(memory_space=pltpu.VMEM)
ANY = pl.BlockSpec(memory_space=pl.ANY)
SMEM = pl.BlockSpec(memory_space=pltpu.SMEM)


def z_shifts(value):
    count = value.shape[0]
    wide = value.astype(F32)
    depth = lax.broadcasted_iota(jnp.int32, (count, W), 0) % Z
    below = jnp.where(depth == 0, 0.0, pltpu.roll(wide, 1, 0)).astype(BF)
    above = jnp.where(depth == Z - 1, 0.0, pltpu.roll(wide, count - 1, 0)).astype(BF)
    return below, value, above


def tap(w, a, b, c):
    lane = (3 * b + c) * C
    return w[a, :, lane : lane + C]


def row_mask(count, first, place):
    row = lax.broadcasted_iota(jnp.int32, (count * Z, W), 0) // Z + (first + ROWS * place)
    return (row >= 0) & (row < SPACE * ROWS)


def conv(value, w, out_rows):
    stacked = jnp.concatenate(z_shifts(value), axis=1)
    total = None
    for a in range(3):
        kernel = jnp.concatenate(
            [
                jnp.concatenate([tap(w, a, y_in - y_out + 1, c) for c in range(3) for y_in in range(Y)], axis=1)
                for y_out in range(Y)
            ],
            axis=0,
        )
        part = lax.dot_general(
            stacked[a * Z : (a + out_rows) * Z],
            kernel,
            (((1,), (1,)), ((), ())),
            preferred_element_type=F32,
        )
        total = part if total is None else total + part
    return total


def conv_adjoint(value, w, out_rows):
    below, same, above = z_shifts(value)
    stacked = jnp.concatenate([above, same, below], axis=1)
    total = None
    for a in range(3):
        kernel = jnp.concatenate(
            [
                jnp.concatenate([tap(w, a, y_in - y_out + 1, c) for y_in in range(Y)], axis=1)
                for c in range(3)
                for y_out in range(Y)
            ],
            axis=0,
        )
        part = jnp.dot(
            stacked[(2 - a) * Z : (2 - a + out_rows) * Z], kernel, preferred_element_type=F32
        )
        total = part if total is None else total + part
    return total


def gated(pre):
    logistic = jax.nn.sigmoid(pre)
    return pre * logistic, logistic * (1.0 + pre * (1.0 - logistic))


def middle(value, halo, keep):
    return value[(halo - keep) * Z : (halo + ROWS + keep) * Z]


def encode_kernel(place_ref, w_ref, bias_ref, far_left, left, own, right, far_right, *outs):
    v_ref, h_ref, s1_ref, s2_ref, out_ref = outs
    inputs = jnp.concatenate(
        [far_left[...], left[...], own[...], right[...], far_right[...]], axis=0
    )
    v_ref[...] = middle(inputs, 6, 1)
    act, slope = gated(conv(inputs, w_ref.at[0], 14) + bias_ref[0:1, :])
    s1_ref[...] = middle(slope, 5, 1)
    act = jnp.where(row_mask(14, -5, place_ref[0]), act, 0.0).astype(BF)
    h_ref[...] = middle(act, 5, 1)
    act, slope = gated(conv(act, w_ref.at[1], 12) + bias_ref[1:2, :])
    s2_ref[...] = middle(slope, 4, 2)
    out_ref[...] = act.astype(BF)


def decode_kernel(place_ref, w_ref, bias_ref, enc_ref, left, own, right, *outs):
    v_ref, h_ref, s1_ref, s2_ref = outs
    place = place_ref[0]
    upper = jnp.concatenate([left[0:CELLS], own[0:CELLS], right[0:CELLS]], axis=0)
    act = enc_ref[...].astype(F32) + upper.astype(F32)
    act = jnp.where(row_mask(12, -4, place), act, 0.0).astype(BF)
    v_ref[...] = middle(act, 4, 1)
    act, slope = gated(conv(act, w_ref.at[2], 10) + bias_ref[2:3, :])
    s1_ref[...] = middle(slope, 3, 1)
    act = jnp.where(row_mask(10, -3, place), act, 0.0).astype(BF)
    h_ref[...] = middle(act, 3, 1)
    _, slope = gated(conv(act, w_ref.at[3], 8) + bias_ref[3:4, :])
    s2_ref[...] = middle(slope, 2, 2)


def sds(rows, dtype):
    return jax.ShapeDtypeStruct((rows * Z, W), dtype)


def forward(kernel, more, *args):
    return pl.pallas_call(
        kernel,
        out_shape=[sds(6, BF), sds(6, BF), sds(6, F32), sds(8, F32)] + more,
        in_specs=[SMEM] + [VMEM] * (len(args) - 1),
        out_specs=[VMEM] * (4 + len(more)),
        compiler_params=pltpu.CompilerParams(vmem_limit_bytes=16 << 20),
        cost_estimate=pl.CostEstimate(flops=3 * 10**9, bytes_accessed=5 << 20, transcendentals=0),
    )(*args)


def tick_kernel(layer, turn, seeded, place_ref, w_ref, *refs):
    names = list(refs)
    s1_ref, s2_ref = names[0:2]
    cots = [names[2:5]]
    rest = names[5:]
    if seeded == "sum":
        cots.append(rest[0:3])
        rest = rest[3:]
    outs = rest[-5:]
    place = place_ref[0]

    def run():
        def window(three):
            low, mid, high = (ref[...] for ref in three)
            return jnp.concatenate([low, mid, high], axis=0)

        g = window(cots[0]).astype(F32)
        if len(cots) > 1:
            g = (g + window(cots[1]).astype(F32)).astype(BF).astype(F32)
        second = (g * s2_ref[...]).astype(BF)
        outs[0][...] = second[2 * Z : 2 * Z + CELLS]
        first = conv_adjoint(second, w_ref.at[layer + 1], 6) * s1_ref[...]
        first = jnp.where(row_mask(6, -1, place), first, 0.0).astype(BF)
        outs[1][...] = first[Z : Z + CELLS]
        grad = conv_adjoint(first, w_ref.at[layer], 4).astype(BF)
        outs[2][...] = grad
        outs[3][...] = grad[0 : 2 * Z]
        outs[4][...] = grad[CELLS - 2 * Z : CELLS]

    if turn is None:
        run()
        return

    def carry():
        for out, ref in zip(outs, rest[:5]):
            out[...] = ref[...]

    mine = place_ref[1] == turn
    pl.when(mine)(run)
    pl.when(jnp.logical_not(mine))(carry)


def tick(layer, turn, place, weights, slopes, cot, skip=None, state=None):
    args = [place, weights, *slopes, *cot]
    seeded = "plain"
    if skip is not None:
        args += list(skip)
        seeded = "sum"
    if state is not None:
        args += list(state)
    return pl.pallas_call(
        lambda *refs: tick_kernel(layer, turn, seeded, *refs),
        out_shape=[sds(4, BF)] * 3 + [sds(2, BF)] * 2,
        in_specs=[SMEM] + [VMEM] * (len(args) - 1),
        out_specs=[VMEM] * 5,
        compiler_params=pltpu.CompilerParams(vmem_limit_bytes=16 << 20),
        cost_estimate=pl.CostEstimate(flops=3 * 10**9, bytes_accessed=4 << 20, transcendentals=0),
        name="tick",
    )(*args)


PARTS = 4
PIECES = 8
USED = 27 * C // PARTS
PIECE = 112
PART = PIECES * PIECE
GRID_AXES = ("section", "space")


def shifted(source_section, by, step):
    pairs = []
    for place in range(SPACE):
        if 0 <= place + step < SPACE:
            source = source_section * SPACE + place
            pairs.append((source, source + by * SPACE + step))
    return pairs


def hand_on(state, source_section, by):
    grad, low, high = state[2:5]
    middle = lax.ppermute(grad, GRID_AXES, shifted(source_section, by, 0))
    before = lax.ppermute(high, GRID_AXES, shifted(source_section, by, 1))
    after = lax.ppermute(low, GRID_AXES, shifted(source_section, by, -1))
    return (before, middle, after)


def beside(array, step):
    pairs = [(place, place + step) for place in range(SPACE) if 0 <= place + step < SPACE]
    return lax.ppermute(array, "space", pairs)


def weight_kernel(group, place_ref, *refs):
    section = place_ref[1]

    @pl.when((section >= group[0]) & (section <= group[-1]))
    def _():
        weight_body(place_ref[0] % 2, *refs)


def weight_body(core, u1_ref, v1_ref, u2_ref, v2_ref, keep_ref, send_ref, held):
    for layer, (u_ref, v_ref) in enumerate(((u1_ref, v1_ref), (u2_ref, v2_ref))):
        grads = u_ref[...]
        wide = grads.astype(F32)
        turned = wide.T.astype(BF)
        stacked = jnp.concatenate(z_shifts(v_ref[...]), axis=1)
        for a in range(3):
            product = jnp.dot(
                turned, stacked[a * Z : a * Z + CELLS], preferred_element_type=F32
            )

            def block(y_out, c, y_in):
                lane = (c * Y + y_in) * C
                return product[y_out * C : (y_out + 1) * C, lane : lane + C]

            for c in range(3):
                blocks = (block(1, c, 0), block(0, c, 0) + block(1, c, 1), block(0, c, 1))
                for b in range(3):
                    value = blocks[b].astype(BF)
                    row = (9 * a + 3 * b + c) * (C // PARTS)
                    for part in range(PARTS):
                        held[layer, part, row : row + C // PARTS, :] = value[
                            part * (C // PARTS) : (part + 1) * (C // PARTS)
                        ]
        sums = jnp.sum(wide, axis=0, keepdims=True)
        sums = sums[:, 0:C] + sums[:, C : 2 * C]
        for part in range(PARTS):
            held[layer, part, USED:PART, :] = jnp.broadcast_to(sums, (PART - USED, C)).astype(BF)
    keep_ref[...] = held[core]
    send_ref[...] = held[1 - core]


def weight_terms(place, group, u1, v1, u2, v2):
    shape = jax.ShapeDtypeStruct((PARTS, PART, C), BF)
    return pl.pallas_call(
        lambda *refs: weight_kernel(group, *refs),
        out_shape=[shape, shape],
        in_specs=[SMEM] + [VMEM] * 4,
        out_specs=[VMEM] * 2,
        scratch_shapes=[pltpu.VMEM((2, PARTS, PART, C), BF)],
        compiler_params=pltpu.CompilerParams(vmem_limit_bytes=16 << 20),
        cost_estimate=pl.CostEstimate(flops=2 * 10**9, bytes_accessed=4 << 20, transcendentals=0),
        name="weights",
    )(place, u1, v1, u2, v2)


def split_kernel(ways, spot, count, place_ref, *refs):
    owns, arrived, outs, total = refs[:count], refs[count : -1 - ways], refs[-1 - ways : -1], refs[-1]
    _, _, rows, _ = total.shape
    if count == 3:
        total[0:1] = owns[0][...].reshape(1, ways, rows, C)

        @pl.when(place_ref[1] < SECTIONS // 2)
        def _():
            total[1:2] = owns[1][...].reshape(1, ways, rows, C)

        @pl.when(place_ref[1] >= SECTIONS // 2)
        def _():
            total[1:2] = owns[2][...].reshape(1, ways, rows, C)
    else:
        value = owns[0][...].astype(F32)
        for more in arrived:
            value = value + more[...].astype(F32)
        total[...] = value.reshape(total.shape)
    here = spot(place_ref[0])
    outs[0][...] = total[:, here]
    for step in range(1, ways):
        outs[step][...] = total[:, (here + step) % ways].astype(BF)


def split(place, owns, arrived, pair, rows, ways, spot):
    return pl.pallas_call(
        lambda *refs: split_kernel(ways, spot, len(owns), *refs),
        out_shape=[jax.ShapeDtypeStruct((pair, rows, C), F32)]
        + [jax.ShapeDtypeStruct((pair, rows, C), BF)] * (ways - 1),
        in_specs=[SMEM] + [VMEM] * (len(owns) + len(arrived)),
        out_specs=[VMEM] * ways,
        scratch_shapes=[pltpu.VMEM((pair, ways, rows, C), F32)],
        compiler_params=pltpu.CompilerParams(vmem_limit_bytes=8 << 20),
        name="split",
    )(place, *owns, *arrived)


def join_kernel(ways, spot, place_ref, *refs):
    here = spot(place_ref[0])
    out = refs[-1]
    for step in range(ways):
        out[:, (here - step + ways) % ways] = refs[step][...]


def join(place, pieces, spot):
    ways = len(pieces)
    pair, rows, _ = pieces[0].shape
    joined = pl.pallas_call(
        lambda *refs: join_kernel(ways, spot, *refs),
        out_shape=jax.ShapeDtypeStruct((pair, ways, rows, C), BF),
        in_specs=[SMEM] + [VMEM] * ways,
        out_specs=VMEM,
        compiler_params=pltpu.CompilerParams(vmem_limit_bytes=8 << 20),
        name="join",
    )(place, *pieces)
    return joined.reshape(pair, ways * rows, C)


def sum_kernel(*refs):
    value = refs[0][...]
    for ref in refs[1:-1]:
        value = value + ref[...].astype(F32)
    refs[-1][...] = value.astype(refs[-1].dtype)


def added(dtype, *args):
    return pl.pallas_call(
        sum_kernel,
        out_shape=jax.ShapeDtypeStruct(args[0].shape, dtype),
        in_specs=[VMEM] * len(args),
        out_specs=VMEM,
        compiler_params=pltpu.CompilerParams(vmem_limit_bytes=8 << 20),
        name="added",
    )(*args)


def y_of(place):
    return (place // 2) % 4


def z_high(place):
    return place // 16


def z_low(place):
    return (place // 8) % 2


def core_step(place, step):
    return place ^ 1


def y_step(place, step):
    return (place // 8) * 8 + ((place // 2 + step) % 4) * 2 + place % 2


def z_high_step(place, step):
    return (place + 16 * step) % SPACE


def z_low_step(place, step):
    return place ^ 8


def send(array, move, step, group=range(SECTIONS)):
    pairs = [
        (section * SPACE + place, section * SPACE + move(place, step))
        for section in group
        for place in range(SPACE)
    ]
    return lax.ppermute(array, GRID_AXES, pairs)


def first_phases(place, terms, group=range(SECTIONS)):
    keep, given = weight_terms(place, group, *terms)
    arrived = [send(given, core_step, 1, group)]
    pieces = split(place, [keep], arrived, 1, PART, PARTS, y_of)
    arrived = [send(pieces[step], y_step, step, group) for step in (2, 1, 3)]
    return added(F32, pieces[0], *arrived)


def last_phases(place, totals):
    pieces = split(place, totals, [], 2, 2 * PIECE, 4, z_high)
    arrived = [send(pieces[step], z_high_step, step) for step in (2, 1, 3)]
    own = added(F32, pieces[0], *arrived)
    pieces = split(place, [own], [], 2, PIECE, 2, z_low)
    whole = added(BF, pieces[0], send(pieces[1], z_low_step, 1))
    whole = join(place, [whole, send(whole, z_low_step, 1)], z_low)
    moved = {step: send(whole, z_high_step, step) for step in (2, 1, 3)}
    own = join_pair(place, [whole] + [moved[step] for step in range(1, 4)])
    behind = [send(part, y_step, 1) for part in own]
    ahead = [send(part, y_step, 3) for part in own]
    across = [send(behind[0], y_step, 1), send(ahead[1], y_step, 3)]
    return [
        join_y(place, [own[half], behind[half], across[half], ahead[half]]) for half in range(2)
    ]


def join_pair_kernel(place_ref, *refs):
    here = z_high(place_ref[0])
    outs = refs[4:]
    for step in range(4):
        for half in range(2):
            outs[half][(here - step + 4) % 4] = refs[step][half]


def join_pair(place, pieces):
    rows = pieces[0].shape[1]
    shape = jax.ShapeDtypeStruct((4, rows, C), BF)
    joined = pl.pallas_call(
        join_pair_kernel,
        out_shape=[shape, shape],
        in_specs=[SMEM] + [VMEM] * 4,
        out_specs=[VMEM] * 2,
        compiler_params=pltpu.CompilerParams(vmem_limit_bytes=8 << 20),
        name="join_pair",
    )(place, *pieces)
    return [part.reshape(4 * rows, C) for part in joined]


def join_y_kernel(place_ref, *refs):
    here = y_of(place_ref[0])
    for step in range(4):
        refs[4][(here - step + 4) % 4] = refs[step][...]


def join_y(place, pieces):
    return pl.pallas_call(
        join_y_kernel,
        out_shape=jax.ShapeDtypeStruct((PARTS, PART, C), BF),
        in_specs=[SMEM] + [VMEM] * 4,
        out_specs=VMEM,
        compiler_params=pltpu.CompilerParams(vmem_limit_bytes=8 << 20),
        name="join_y",
    )(place, *pieces)


def unpack_kernel(place_ref, enc_ref, dec_ref, *refs):
    weight_ref, bias_ref = refs[-2:]

    def write(ref):
        def one(index, carry):
            part, a = index // 3, index % 3
            rows = pl.ds(pl.multiple_of(part * (C // PARTS), C // PARTS), C // PARTS)
            for j in range(9):
                row = pl.multiple_of((9 * a + j) * (C // PARTS), C // PARTS)
                weight_ref[0, a, rows, j * C : (j + 1) * C] = ref[
                    part, pl.ds(row, C // PARTS), :
                ].astype(F32)
            return carry

        lax.fori_loop(0, 3 * PARTS, one, 0)
        bias_ref[0] = ref[0, USED : USED + 16, :].astype(F32)[0:1]

    encoder = pl.program_id(0) == 0
    pl.when(encoder)(lambda: write(enc_ref))
    pl.when(jnp.logical_not(encoder))(lambda: write(dec_ref))


def unpack(place, flip, parts, onto=()):
    def spot(block, place_ref):
        return 2 * block + (place_ref[0] + flip) % 2

    return pl.pallas_call(
        lambda *refs: unpack_kernel(*refs),
        out_shape=[
            jax.ShapeDtypeStruct((4, 3, C, 9 * C), F32),
            jax.ShapeDtypeStruct((4, 1, C), F32),
        ],
        grid_spec=pltpu.PrefetchScalarGridSpec(
            num_scalar_prefetch=1,
            grid=(2,),
            in_specs=[VMEM] * 2 + [ANY] * len(onto),
            out_specs=[
                pl.BlockSpec((1, 3, C, 9 * C), lambda *at: (spot(*at), 0, 0, 0)),
                pl.BlockSpec((1, 1, C), lambda *at: (spot(*at), 0, 0)),
            ],
        ),
        input_output_aliases={3 + index: index for index in range(len(onto))},
        compiler_params=pltpu.CompilerParams(vmem_limit_bytes=16 << 20),
        name="unpack",
    )(place, *parts, *onto)


def to_cells(block):
    return block.transpose(1, 3, 2, 0).reshape(CELLS, W)


def from_cells(field):
    return field.reshape(ROWS, Z, Y, C).transpose(3, 0, 2, 1)[None, None]


def whole_pass(encoder_inputs, upper_inputs, output_cotangent, weights, biases):
    section = lax.axis_index("section")
    space = lax.axis_index("space")
    place = jnp.stack([space, section]).astype(jnp.int32)
    kernels = weights[0]
    bias_rows = jnp.concatenate([biases[0], biases[0]], axis=1)
    enc = to_cells(encoder_inputs[0, 0])
    far_left = beside(enc[CELLS - 2 * Z :], 2)
    far_right = beside(enc[: 2 * Z], -2)
    left = beside(enc, 1)
    right = beside(enc, -1)
    rest = jnp.concatenate([to_cells(upper_inputs[0, 0]), to_cells(output_cotangent[0])], axis=0)
    rest_left = beside(rest, 1)
    rest_right = beside(rest, -1)
    enc_v, enc_h, enc_s1, enc_s2, enc_out = forward(
        encode_kernel, [sds(12, BF)],
        place, kernels, bias_rows, far_left, left, enc, right, far_right,
    )
    dec_v, dec_h, dec_s1, dec_s2 = forward(
        decode_kernel, [],
        place, kernels, bias_rows, enc_out, rest_left, rest, rest_right,
    )
    cot = (
        rest_left[2 * CELLS - 2 * Z :],
        rest[CELLS:],
        rest_right[CELLS : CELLS + 2 * Z],
    )
    slopes = (dec_s1, dec_s2)
    state = tick(2, None, place, kernels, slopes, cot)
    near = far = None
    for turn in range(1, SECTIONS):
        cot = hand_on(state, turn - 1, 1)
        if turn == 3:
            near = first_phases(place, (state[1], dec_v, state[0], dec_h), range(0, 2))
        state = tick(2, turn, place, kernels, slopes, cot, state=state)
    upper = state
    skip = (beside(upper[4], 1), upper[2], beside(upper[3], -1))
    slopes = (enc_s1, enc_s2)
    state = tick(0, None, place, kernels, slopes, skip)
    for turn in range(SECTIONS - 2, -1, -1):
        cot = hand_on(state, turn + 1, -1)
        if turn == 1:
            far = first_phases(place, (upper[1], dec_v, upper[0], dec_h), range(2, 4))
        state = tick(0, turn, place, kernels, slopes, cot, skip=skip, state=state)
    enc_total = first_phases(place, (state[1], enc_v, state[0], enc_h))
    mine = last_phases(place, [enc_total, near, far])
    other = [send(part, core_step, 1) for part in mine]
    totals = unpack(place, 0, mine)
    weight_total, bias_total = unpack(place, 1, other, totals)
    return (
        from_cells(state[2]),
        from_cells(upper[2]),
        weight_total[None],
        bias_total.reshape(1, 4, C),
    )


def solution(mesh):
    return jax.shard_map(
        whole_pass,
        mesh=mesh,
        in_specs=(
            P("section", None, None, "space", None, None),
            P("section", None, None, "space", None, None),
            P(None, None, "space", None, None),
            P("section", None, None, None, None),
            P("section", None, None),
        ),
        out_specs=(
            P("section", None, None, "space", None, None),
            P("section", None, None, "space", None, None),
            P("section", None, None, None, None),
            P("section", None, None),
        ),
        check_vma=False,
    )
```

```python
import jax
import jax.numpy as jnp
from jax import lax
from jax.experimental import pallas as pl
from jax.experimental.pallas import tpu as pltpu
from jax.sharding import PartitionSpec as P


C = 128
Y = 2
Z = 64
W = Y * C
SPACE = 64
SECTIONS = 4
ROWS = 4
CELLS = ROWS * Z
BF = jnp.bfloat16
F32 = jnp.float32
VMEM = pl.BlockSpec(memory_space=pltpu.VMEM)
ANY = pl.BlockSpec(memory_space=pl.ANY)
SMEM = pl.BlockSpec(memory_space=pltpu.SMEM)


def z_shifts(value):
    count = value.shape[0]
    wide = value.astype(F32)
    depth = lax.broadcasted_iota(jnp.int32, (count, W), 0) % Z
    below = jnp.where(depth == 0, 0.0, pltpu.roll(wide, 1, 0)).astype(BF)
    above = jnp.where(depth == Z - 1, 0.0, pltpu.roll(wide, count - 1, 0)).astype(BF)
    return below, value, above


def tap(w, a, b, c):
    lane = (3 * b + c) * C
    return w[a, :, lane : lane + C]


def row_mask(count, first, place):
    row = lax.broadcasted_iota(jnp.int32, (count * Z, W), 0) // Z + (first + ROWS * place)
    return (row >= 0) & (row < SPACE * ROWS)


def conv(value, w, out_rows):
    stacked = jnp.concatenate(z_shifts(value), axis=1)
    total = None
    for a in range(3):
        kernel = jnp.concatenate(
            [
                jnp.concatenate([tap(w, a, y_in - y_out + 1, c) for c in range(3) for y_in in range(Y)], axis=1)
                for y_out in range(Y)
            ],
            axis=0,
        )
        part = lax.dot_general(
            stacked[a * Z : (a + out_rows) * Z],
            kernel,
            (((1,), (1,)), ((), ())),
            preferred_element_type=F32,
        )
        total = part if total is None else total + part
    return total


def conv_adjoint(value, w, out_rows):
    below, same, above = z_shifts(value)
    stacked = jnp.concatenate([above, same, below], axis=1)
    total = None
    for a in range(3):
        kernel = jnp.concatenate(
            [
                jnp.concatenate([tap(w, a, y_in - y_out + 1, c) for y_in in range(Y)], axis=1)
                for c in range(3)
                for y_out in range(Y)
            ],
            axis=0,
        )
        part = jnp.dot(
            stacked[(2 - a) * Z : (2 - a + out_rows) * Z], kernel, preferred_element_type=F32
        )
        total = part if total is None else total + part
    return total


def gated(pre):
    logistic = jax.nn.sigmoid(pre)
    return pre * logistic, logistic * (1.0 + pre * (1.0 - logistic))


def middle(value, halo, keep):
    return value[(halo - keep) * Z : (halo + ROWS + keep) * Z]


def encode_kernel(place_ref, w_ref, bias_ref, far_left, left, own, right, far_right, *outs):
    v_ref, h_ref, s1_ref, s2_ref, out_ref = outs
    inputs = jnp.concatenate(
        [far_left[...], left[...], own[...], right[...], far_right[...]], axis=0
    )
    v_ref[...] = middle(inputs, 6, 1)
    act, slope = gated(conv(inputs, w_ref.at[0], 14) + bias_ref[0:1, :])
    s1_ref[...] = middle(slope, 5, 1)
    act = jnp.where(row_mask(14, -5, place_ref[0]), act, 0.0).astype(BF)
    h_ref[...] = middle(act, 5, 1)
    act, slope = gated(conv(act, w_ref.at[1], 12) + bias_ref[1:2, :])
    s2_ref[...] = middle(slope, 4, 2)
    out_ref[...] = act.astype(BF)


def decode_kernel(place_ref, w_ref, bias_ref, enc_ref, left, own, right, *outs):
    v_ref, h_ref, s1_ref, s2_ref = outs
    place = place_ref[0]
    upper = jnp.concatenate([left[0:CELLS], own[0:CELLS], right[0:CELLS]], axis=0)
    act = enc_ref[...].astype(F32) + upper.astype(F32)
    act = jnp.where(row_mask(12, -4, place), act, 0.0).astype(BF)
    v_ref[...] = middle(act, 4, 1)
    act, slope = gated(conv(act, w_ref.at[2], 10) + bias_ref[2:3, :])
    s1_ref[...] = middle(slope, 3, 1)
    act = jnp.where(row_mask(10, -3, place), act, 0.0).astype(BF)
    h_ref[...] = middle(act, 3, 1)
    _, slope = gated(conv(act, w_ref.at[3], 8) + bias_ref[3:4, :])
    s2_ref[...] = middle(slope, 2, 2)


def sds(rows, dtype):
    return jax.ShapeDtypeStruct((rows * Z, W), dtype)


def forward(kernel, more, *args):
    return pl.pallas_call(
        kernel,
        out_shape=[sds(6, BF), sds(6, BF), sds(6, F32), sds(8, F32)] + more,
        in_specs=[SMEM] + [VMEM] * (len(args) - 1),
        out_specs=[VMEM] * (4 + len(more)),
        compiler_params=pltpu.CompilerParams(vmem_limit_bytes=16 << 20),
        cost_estimate=pl.CostEstimate(flops=3 * 10**9, bytes_accessed=5 << 20, transcendentals=0),
    )(*args)


def tick_kernel(layer, turn, seeded, place_ref, w_ref, *refs):
    names = list(refs)
    s1_ref, s2_ref = names[0:2]
    cots = [names[2:5]]
    rest = names[5:]
    if seeded == "sum":
        cots.append(rest[0:3])
        rest = rest[3:]
    outs = rest[-5:]
    place = place_ref[0]

    def run():
        def window(three):
            low, mid, high = (ref[...] for ref in three)
            return jnp.concatenate([low, mid, high], axis=0)

        g = window(cots[0]).astype(F32)
        if len(cots) > 1:
            g = (g + window(cots[1]).astype(F32)).astype(BF).astype(F32)
        second = (g * s2_ref[...]).astype(BF)
        outs[0][...] = second[2 * Z : 2 * Z + CELLS]
        first = conv_adjoint(second, w_ref.at[layer + 1], 6) * s1_ref[...]
        first = jnp.where(row_mask(6, -1, place), first, 0.0).astype(BF)
        outs[1][...] = first[Z : Z + CELLS]
        grad = conv_adjoint(first, w_ref.at[layer], 4).astype(BF)
        outs[2][...] = grad
        outs[3][...] = grad[0 : 2 * Z]
        outs[4][...] = grad[CELLS - 2 * Z : CELLS]

    if turn is None:
        run()
        return

    def carry():
        for out, ref in zip(outs, rest[:5]):
            out[...] = ref[...]

    mine = place_ref[1] == turn
    pl.when(mine)(run)
    pl.when(jnp.logical_not(mine))(carry)


def tick(layer, turn, place, weights, slopes, cot, skip=None, state=None):
    args = [place, weights, *slopes, *cot]
    seeded = "plain"
    if skip is not None:
        args += list(skip)
        seeded = "sum"
    if state is not None:
        args += list(state)
    return pl.pallas_call(
        lambda *refs: tick_kernel(layer, turn, seeded, *refs),
        out_shape=[sds(4, BF)] * 3 + [sds(2, BF)] * 2,
        in_specs=[SMEM] + [VMEM] * (len(args) - 1),
        out_specs=[VMEM] * 5,
        compiler_params=pltpu.CompilerParams(vmem_limit_bytes=16 << 20),
        cost_estimate=pl.CostEstimate(flops=3 * 10**9, bytes_accessed=4 << 20, transcendentals=0),
        name="tick",
    )(*args)


PARTS = 4
PIECES = 8
USED = 27 * C // PARTS
PIECE = 112
PART = PIECES * PIECE
GRID_AXES = ("section", "space")


def shifted(source_section, by, step):
    pairs = []
    for place in range(SPACE):
        if 0 <= place + step < SPACE:
            source = source_section * SPACE + place
            pairs.append((source, source + by * SPACE + step))
    return pairs


def hand_on(state, source_section, by):
    grad, low, high = state[2:5]
    middle = lax.ppermute(grad, GRID_AXES, shifted(source_section, by, 0))
    before = lax.ppermute(high, GRID_AXES, shifted(source_section, by, 1))
    after = lax.ppermute(low, GRID_AXES, shifted(source_section, by, -1))
    return (before, middle, after)


def beside(array, step):
    pairs = [(place, place + step) for place in range(SPACE) if 0 <= place + step < SPACE]
    return lax.ppermute(array, "space", pairs)


def weight_kernel(place_ref, u1_ref, v1_ref, u2_ref, v2_ref, keep_ref, send_ref, held):
    core = place_ref[0] % 2
    for layer, (u_ref, v_ref) in enumerate(((u1_ref, v1_ref), (u2_ref, v2_ref))):
        grads = u_ref[...]
        wide = grads.astype(F32)
        turned = wide.T.astype(BF)
        stacked = jnp.concatenate(z_shifts(v_ref[...]), axis=1)
        for a in range(3):
            product = jnp.dot(
                turned, stacked[a * Z : a * Z + CELLS], preferred_element_type=F32
            )

            def block(y_out, c, y_in):
                lane = (c * Y + y_in) * C
                return product[y_out * C : (y_out + 1) * C, lane : lane + C]

            for c in range(3):
                blocks = (block(1, c, 0), block(0, c, 0) + block(1, c, 1), block(0, c, 1))
                for b in range(3):
                    value = blocks[b].astype(BF)
                    row = (9 * a + 3 * b + c) * (C // PARTS)
                    for part in range(PARTS):
                        held[layer, part, row : row + C // PARTS, :] = value[
                            part * (C // PARTS) : (part + 1) * (C // PARTS)
                        ]
        sums = jnp.sum(wide, axis=0, keepdims=True)
        sums = sums[:, 0:C] + sums[:, C : 2 * C]
        for part in range(PARTS):
            held[layer, part, USED:PART, :] = jnp.broadcast_to(sums, (PART - USED, C)).astype(BF)
    keep_ref[...] = held[core]
    send_ref[...] = held[1 - core]


def weight_terms(place, u1, v1, u2, v2):
    shape = jax.ShapeDtypeStruct((PARTS, PART, C), BF)
    return pl.pallas_call(
        weight_kernel,
        out_shape=[shape, shape],
        in_specs=[SMEM] + [VMEM] * 4,
        out_specs=[VMEM] * 2,
        scratch_shapes=[pltpu.VMEM((2, PARTS, PART, C), BF)],
        compiler_params=pltpu.CompilerParams(vmem_limit_bytes=16 << 20),
        cost_estimate=pl.CostEstimate(flops=2 * 10**9, bytes_accessed=4 << 20, transcendentals=0),
        name="weights",
    )(place, u1, v1, u2, v2)


def split_kernel(ways, spot, count, place_ref, *refs):
    owns, arrived, outs, total = refs[:count], refs[count : -1 - ways], refs[-1 - ways : -1], refs[-1]
    pair, _, rows, _ = total.shape
    for index, ref in enumerate(owns):
        value = ref[...].astype(F32)
        for more in arrived:
            value = value + more[...].astype(F32)
        value = value.reshape(pair // count, ways, rows, C)
        total[index * (pair // count) : (index + 1) * (pair // count)] = value
    here = spot(place_ref[0])
    outs[0][...] = total[:, here]
    for step in range(1, ways):
        outs[step][...] = total[:, (here + step) % ways].astype(BF)


def split(place, owns, arrived, pair, rows, ways, spot):
    return pl.pallas_call(
        lambda *refs: split_kernel(ways, spot, len(owns), *refs),
        out_shape=[jax.ShapeDtypeStruct((pair, rows, C), F32)]
        + [jax.ShapeDtypeStruct((pair, rows, C), BF)] * (ways - 1),
        in_specs=[SMEM] + [VMEM] * (len(owns) + len(arrived)),
        out_specs=[VMEM] * ways,
        scratch_shapes=[pltpu.VMEM((pair, ways, rows, C), F32)],
        compiler_params=pltpu.CompilerParams(vmem_limit_bytes=8 << 20),
        name="split",
    )(place, *owns, *arrived)


def join_kernel(ways, spot, place_ref, *refs):
    here = spot(place_ref[0])
    out = refs[-1]
    for step in range(ways):
        out[:, (here - step + ways) % ways] = refs[step][...]


def join(place, pieces, spot):
    ways = len(pieces)
    pair, rows, _ = pieces[0].shape
    joined = pl.pallas_call(
        lambda *refs: join_kernel(ways, spot, *refs),
        out_shape=jax.ShapeDtypeStruct((pair, ways, rows, C), BF),
        in_specs=[SMEM] + [VMEM] * ways,
        out_specs=VMEM,
        compiler_params=pltpu.CompilerParams(vmem_limit_bytes=8 << 20),
        name="join",
    )(place, *pieces)
    return joined.reshape(pair, ways * rows, C)


def sum_kernel(*refs):
    value = refs[0][...]
    for ref in refs[1:-1]:
        value = value + ref[...].astype(F32)
    refs[-1][...] = value.astype(refs[-1].dtype)


def added(dtype, *args):
    return pl.pallas_call(
        sum_kernel,
        out_shape=jax.ShapeDtypeStruct(args[0].shape, dtype),
        in_specs=[VMEM] * len(args),
        out_specs=VMEM,
        compiler_params=pltpu.CompilerParams(vmem_limit_bytes=8 << 20),
        name="added",
    )(*args)


def y_of(place):
    return (place // 2) % 4


def z_high(place):
    return place // 16


def z_low(place):
    return (place // 8) % 2


def core_step(place, step):
    return place ^ 1


def y_step(place, step):
    return (place // 8) * 8 + ((place // 2 + step) % 4) * 2 + place % 2


def z_high_step(place, step):
    return (place + 16 * step) % SPACE


def z_low_step(place, step):
    return place ^ 8


def send(array, move, step):
    return lax.ppermute(array, "space", [(place, move(place, step)) for place in range(SPACE)])


def first_phases(place, terms):
    keep, given = weight_terms(place, *terms)
    arrived = [send(given, core_step, 1)]
    pieces = split(place, [keep], arrived, 1, PART, PARTS, y_of)
    arrived = [send(pieces[step], y_step, step) for step in (2, 1, 3)]
    return added(F32, pieces[0], *arrived)


def last_phases(place, totals):
    pieces = split(place, totals, [], 2, 2 * PIECE, 4, z_high)
    arrived = [send(pieces[step], z_high_step, step) for step in (2, 1, 3)]
    own = added(F32, pieces[0], *arrived)
    pieces = split(place, [own], [], 2, PIECE, 2, z_low)
    whole = added(BF, pieces[0], send(pieces[1], z_low_step, 1))
    whole = join(place, [whole, send(whole, z_low_step, 1)], z_low)
    moved = {step: send(whole, z_high_step, step) for step in (2, 1, 3)}
    own = join_pair(place, [whole] + [moved[step] for step in range(1, 4)])
    behind = [send(part, y_step, 1) for part in own]
    ahead = [send(part, y_step, 3) for part in own]
    across = [send(behind[0], y_step, 1), send(ahead[1], y_step, 3)]
    return [
        join_y(place, [own[half], behind[half], across[half], ahead[half]]) for half in range(2)
    ]


def join_pair_kernel(place_ref, *refs):
    here = z_high(place_ref[0])
    outs = refs[4:]
    for step in range(4):
        for half in range(2):
            outs[half][(here - step + 4) % 4] = refs[step][half]


def join_pair(place, pieces):
    rows = pieces[0].shape[1]
    shape = jax.ShapeDtypeStruct((4, rows, C), BF)
    joined = pl.pallas_call(
        join_pair_kernel,
        out_shape=[shape, shape],
        in_specs=[SMEM] + [VMEM] * 4,
        out_specs=[VMEM] * 2,
        compiler_params=pltpu.CompilerParams(vmem_limit_bytes=8 << 20),
        name="join_pair",
    )(place, *pieces)
    return [part.reshape(4 * rows, C) for part in joined]


def join_y_kernel(place_ref, *refs):
    here = y_of(place_ref[0])
    for step in range(4):
        refs[4][(here - step + 4) % 4] = refs[step][...]


def join_y(place, pieces):
    return pl.pallas_call(
        join_y_kernel,
        out_shape=jax.ShapeDtypeStruct((PARTS, PART, C), BF),
        in_specs=[SMEM] + [VMEM] * 4,
        out_specs=VMEM,
        compiler_params=pltpu.CompilerParams(vmem_limit_bytes=8 << 20),
        name="join_y",
    )(place, *pieces)


def unpack_kernel(place_ref, enc_ref, dec_ref, *refs):
    weight_ref, bias_ref = refs[-2:]

    def write(ref):
        def one(index, carry):
            part, a = index // 3, index % 3
            rows = pl.ds(pl.multiple_of(part * (C // PARTS), C // PARTS), C // PARTS)
            for j in range(9):
                row = pl.multiple_of((9 * a + j) * (C // PARTS), C // PARTS)
                weight_ref[0, a, rows, j * C : (j + 1) * C] = ref[
                    part, pl.ds(row, C // PARTS), :
                ].astype(F32)
            return carry

        lax.fori_loop(0, 3 * PARTS, one, 0)
        bias_ref[0] = ref[0, USED : USED + 16, :].astype(F32)[0:1]

    encoder = pl.program_id(0) == 0
    pl.when(encoder)(lambda: write(enc_ref))
    pl.when(jnp.logical_not(encoder))(lambda: write(dec_ref))


def unpack(place, flip, parts, onto=()):
    def spot(block, place_ref):
        return 2 * block + (place_ref[0] + flip) % 2

    return pl.pallas_call(
        lambda *refs: unpack_kernel(*refs),
        out_shape=[
            jax.ShapeDtypeStruct((4, 3, C, 9 * C), F32),
            jax.ShapeDtypeStruct((4, 1, C), F32),
        ],
        grid_spec=pltpu.PrefetchScalarGridSpec(
            num_scalar_prefetch=1,
            grid=(2,),
            in_specs=[VMEM] * 2 + [ANY] * len(onto),
            out_specs=[
                pl.BlockSpec((1, 3, C, 9 * C), lambda *at: (spot(*at), 0, 0, 0)),
                pl.BlockSpec((1, 1, C), lambda *at: (spot(*at), 0, 0)),
            ],
        ),
        input_output_aliases={3 + index: index for index in range(len(onto))},
        compiler_params=pltpu.CompilerParams(vmem_limit_bytes=16 << 20),
        name="unpack",
    )(place, *parts, *onto)


def to_cells(block):
    return block.transpose(1, 3, 2, 0).reshape(CELLS, W)


def from_cells(field):
    return field.reshape(ROWS, Z, Y, C).transpose(3, 0, 2, 1)[None, None]


def whole_pass(encoder_inputs, upper_inputs, output_cotangent, weights, biases):
    section = lax.axis_index("section")
    space = lax.axis_index("space")
    place = jnp.stack([space, section]).astype(jnp.int32)
    kernels = weights[0]
    bias_rows = jnp.concatenate([biases[0], biases[0]], axis=1)
    enc = to_cells(encoder_inputs[0, 0])
    far_left = beside(enc[CELLS - 2 * Z :], 2)
    far_right = beside(enc[: 2 * Z], -2)
    left = beside(enc, 1)
    right = beside(enc, -1)
    rest = jnp.concatenate([to_cells(upper_inputs[0, 0]), to_cells(output_cotangent[0])], axis=0)
    rest_left = beside(rest, 1)
    rest_right = beside(rest, -1)
    enc_v, enc_h, enc_s1, enc_s2, enc_out = forward(
        encode_kernel, [sds(12, BF)],
        place, kernels, bias_rows, far_left, left, enc, right, far_right,
    )
    dec_v, dec_h, dec_s1, dec_s2 = forward(
        decode_kernel, [],
        place, kernels, bias_rows, enc_out, rest_left, rest, rest_right,
    )
    cot = (
        rest_left[2 * CELLS - 2 * Z :],
        rest[CELLS:],
        rest_right[CELLS : CELLS + 2 * Z],
    )
    slopes = (dec_s1, dec_s2)
    state = tick(2, None, place, kernels, slopes, cot)
    for turn in range(1, SECTIONS):
        cot = hand_on(state, turn - 1, 1)
        state = tick(2, turn, place, kernels, slopes, cot, state=state)
    upper = state
    skip = (beside(upper[4], 1), upper[2], beside(upper[3], -1))
    slopes = (enc_s1, enc_s2)
    state = tick(0, None, place, kernels, slopes, skip)
    for turn in range(SECTIONS - 2, -1, -1):
        cot = hand_on(state, turn + 1, -1)
        if turn == 1:
            dec_total = first_phases(place, (upper[1], dec_v, upper[0], dec_h))
        state = tick(0, turn, place, kernels, slopes, cot, skip=skip, state=state)
    enc_total = first_phases(place, (state[1], enc_v, state[0], enc_h))
    mine = last_phases(place, [enc_total, dec_total])
    other = [send(part, core_step, 1) for part in mine]
    totals = unpack(place, 0, mine)
    weight_total, bias_total = unpack(place, 1, other, totals)
    return (
        from_cells(state[2]),
        from_cells(upper[2]),
        weight_total[None],
        bias_total.reshape(1, 4, C),
    )


def solution(mesh):
    return jax.shard_map(
        whole_pass,
        mesh=mesh,
        in_specs=(
            P("section", None, None, "space", None, None),
            P("section", None, None, "space", None, None),
            P(None, None, "space", None, None),
            P("section", None, None, None, None),
            P("section", None, None),
        ),
        out_specs=(
            P("section", None, None, "space", None, None),
            P("section", None, None, "space", None, None),
            P("section", None, None, None, None),
            P("section", None, None),
        ),
        check_vma=False,
    )
```

```python
import jax
import jax.numpy as jnp
from jax import lax
from jax.experimental import pallas as pl
from jax.experimental.pallas import tpu as pltpu
from jax.sharding import PartitionSpec as P


C = 128
Y = 2
Z = 64
W = Y * C
SPACE = 64
SECTIONS = 4
ROWS = 4
CELLS = ROWS * Z
BF = jnp.bfloat16
F32 = jnp.float32
VMEM = pl.BlockSpec(memory_space=pltpu.VMEM)
ANY = pl.BlockSpec(memory_space=pl.ANY)
SMEM = pl.BlockSpec(memory_space=pltpu.SMEM)


def z_shifts(value):
    count = value.shape[0]
    wide = value.astype(F32)
    depth = lax.broadcasted_iota(jnp.int32, (count, W), 0) % Z
    below = jnp.where(depth == 0, 0.0, pltpu.roll(wide, 1, 0)).astype(BF)
    above = jnp.where(depth == Z - 1, 0.0, pltpu.roll(wide, count - 1, 0)).astype(BF)
    return below, value, above


def tap(w, a, b, c):
    lane = (3 * b + c) * C
    return w[a, :, lane : lane + C]


def row_mask(count, first, place):
    row = lax.broadcasted_iota(jnp.int32, (count * Z, W), 0) // Z + (first + ROWS * place)
    return (row >= 0) & (row < SPACE * ROWS)


def conv(value, w, out_rows):
    stacked = jnp.concatenate(z_shifts(value), axis=1)
    total = None
    for a in range(3):
        kernel = jnp.concatenate(
            [
                jnp.concatenate([tap(w, a, y_in - y_out + 1, c) for c in range(3) for y_in in range(Y)], axis=1)
                for y_out in range(Y)
            ],
            axis=0,
        )
        part = lax.dot_general(
            stacked[a * Z : (a + out_rows) * Z],
            kernel,
            (((1,), (1,)), ((), ())),
            preferred_element_type=F32,
        )
        total = part if total is None else total + part
    return total


def conv_adjoint(value, w, out_rows):
    below, same, above = z_shifts(value)
    stacked = jnp.concatenate([above, same, below], axis=1)
    total = None
    for a in range(3):
        kernel = jnp.concatenate(
            [
                jnp.concatenate([tap(w, a, y_in - y_out + 1, c) for y_in in range(Y)], axis=1)
                for c in range(3)
                for y_out in range(Y)
            ],
            axis=0,
        )
        part = jnp.dot(
            stacked[(2 - a) * Z : (2 - a + out_rows) * Z], kernel, preferred_element_type=F32
        )
        total = part if total is None else total + part
    return total


def gated(pre):
    logistic = jax.nn.sigmoid(pre)
    return pre * logistic, logistic * (1.0 + pre * (1.0 - logistic))


def middle(value, halo, keep):
    return value[(halo - keep) * Z : (halo + ROWS + keep) * Z]


def encode_kernel(place_ref, w_ref, bias_ref, far_left, left, own, right, far_right, *outs):
    v_ref, h_ref, s1_ref, s2_ref, out_ref = outs
    inputs = jnp.concatenate(
        [far_left[...], left[...], own[...], right[...], far_right[...]], axis=0
    )
    v_ref[...] = middle(inputs, 6, 1)
    act, slope = gated(conv(inputs, w_ref.at[0], 14) + bias_ref[0:1, :])
    s1_ref[...] = middle(slope, 5, 1)
    act = jnp.where(row_mask(14, -5, place_ref[0]), act, 0.0).astype(BF)
    h_ref[...] = middle(act, 5, 1)
    act, slope = gated(conv(act, w_ref.at[1], 12) + bias_ref[1:2, :])
    s2_ref[...] = middle(slope, 4, 2)
    out_ref[...] = act.astype(BF)


def decode_kernel(place_ref, w_ref, bias_ref, enc_ref, left, own, right, *outs):
    v_ref, h_ref, s1_ref, s2_ref = outs
    place = place_ref[0]
    upper = jnp.concatenate([left[0:CELLS], own[0:CELLS], right[0:CELLS]], axis=0)
    act = enc_ref[...].astype(F32) + upper.astype(F32)
    act = jnp.where(row_mask(12, -4, place), act, 0.0).astype(BF)
    v_ref[...] = middle(act, 4, 1)
    act, slope = gated(conv(act, w_ref.at[2], 10) + bias_ref[2:3, :])
    s1_ref[...] = middle(slope, 3, 1)
    act = jnp.where(row_mask(10, -3, place), act, 0.0).astype(BF)
    h_ref[...] = middle(act, 3, 1)
    _, slope = gated(conv(act, w_ref.at[3], 8) + bias_ref[3:4, :])
    s2_ref[...] = middle(slope, 2, 2)


def sds(rows, dtype):
    return jax.ShapeDtypeStruct((rows * Z, W), dtype)


def forward(kernel, more, *args):
    return pl.pallas_call(
        kernel,
        out_shape=[sds(6, BF), sds(6, BF), sds(6, F32), sds(8, F32)] + more,
        in_specs=[SMEM] + [VMEM] * (len(args) - 1),
        out_specs=[VMEM] * (4 + len(more)),
        compiler_params=pltpu.CompilerParams(vmem_limit_bytes=16 << 20),
        cost_estimate=pl.CostEstimate(flops=3 * 10**9, bytes_accessed=5 << 20, transcendentals=0),
    )(*args)


def tick_kernel(layer, turn, seeded, place_ref, w_ref, *refs):
    names = list(refs)
    s1_ref, s2_ref = names[0:2]
    cots = [names[2:5]]
    rest = names[5:]
    if seeded == "sum":
        cots.append(rest[0:3])
        rest = rest[3:]
    outs = rest[-5:]
    place = place_ref[0]

    def run():
        def window(three):
            low, mid, high = (ref[...] for ref in three)
            return jnp.concatenate([low, mid, high], axis=0)

        g = window(cots[0]).astype(F32)
        if len(cots) > 1:
            g = (g + window(cots[1]).astype(F32)).astype(BF).astype(F32)
        second = (g * s2_ref[...]).astype(BF)
        outs[0][...] = second[2 * Z : 2 * Z + CELLS]
        first = conv_adjoint(second, w_ref.at[layer + 1], 6) * s1_ref[...]
        first = jnp.where(row_mask(6, -1, place), first, 0.0).astype(BF)
        outs[1][...] = first[Z : Z + CELLS]
        grad = conv_adjoint(first, w_ref.at[layer], 4).astype(BF)
        outs[2][...] = grad
        outs[3][...] = grad[0 : 2 * Z]
        outs[4][...] = grad[CELLS - 2 * Z : CELLS]

    if turn is None:
        run()
        return

    def carry():
        for out, ref in zip(outs, rest[:5]):
            out[...] = ref[...]

    mine = place_ref[1] == turn
    pl.when(mine)(run)
    pl.when(jnp.logical_not(mine))(carry)


def tick(layer, turn, place, weights, slopes, cot, skip=None, state=None):
    args = [place, weights, *slopes, *cot]
    seeded = "plain"
    if skip is not None:
        args += list(skip)
        seeded = "sum"
    if state is not None:
        args += list(state)
    return pl.pallas_call(
        lambda *refs: tick_kernel(layer, turn, seeded, *refs),
        out_shape=[sds(4, BF)] * 3 + [sds(2, BF)] * 2,
        in_specs=[SMEM] + [VMEM] * (len(args) - 1),
        out_specs=[VMEM] * 5,
        compiler_params=pltpu.CompilerParams(vmem_limit_bytes=16 << 20),
        cost_estimate=pl.CostEstimate(flops=3 * 10**9, bytes_accessed=4 << 20, transcendentals=0),
        name="tick",
    )(*args)


PARTS = 4
PIECES = 8
USED = 27 * C // PARTS
PIECE = 112
PART = PIECES * PIECE
GRID_AXES = ("section", "space")


def shifted(source_section, by, step):
    pairs = []
    for place in range(SPACE):
        if 0 <= place + step < SPACE:
            source = source_section * SPACE + place
            pairs.append((source, source + by * SPACE + step))
    return pairs


def hand_on(state, source_section, by):
    grad, low, high = state[2:5]
    middle = lax.ppermute(grad, GRID_AXES, shifted(source_section, by, 0))
    before = lax.ppermute(high, GRID_AXES, shifted(source_section, by, 1))
    after = lax.ppermute(low, GRID_AXES, shifted(source_section, by, -1))
    return (before, middle, after)


def beside(array, step):
    pairs = [(place, place + step) for place in range(SPACE) if 0 <= place + step < SPACE]
    return lax.ppermute(array, "space", pairs)


def weight_kernel(place_ref, u1_ref, v1_ref, u2_ref, v2_ref, keep_ref, send_ref, held):
    core = place_ref[0] % 2
    for layer, (u_ref, v_ref) in enumerate(((u1_ref, v1_ref), (u2_ref, v2_ref))):
        grads = u_ref[...]
        wide = grads.astype(F32)
        turned = wide.T.astype(BF)
        stacked = jnp.concatenate(z_shifts(v_ref[...]), axis=1)
        for a in range(3):
            product = jnp.dot(
                turned, stacked[a * Z : a * Z + CELLS], preferred_element_type=F32
            )

            def block(y_out, c, y_in):
                lane = (c * Y + y_in) * C
                return product[y_out * C : (y_out + 1) * C, lane : lane + C]

            for c in range(3):
                blocks = (block(1, c, 0), block(0, c, 0) + block(1, c, 1), block(0, c, 1))
                for b in range(3):
                    value = blocks[b].astype(BF)
                    row = (9 * a + 3 * b + c) * (C // PARTS)
                    for part in range(PARTS):
                        held[layer, part, row : row + C // PARTS, :] = value[
                            part * (C // PARTS) : (part + 1) * (C // PARTS)
                        ]
        sums = jnp.sum(wide, axis=0, keepdims=True)
        sums = sums[:, 0:C] + sums[:, C : 2 * C]
        for part in range(PARTS):
            held[layer, part, USED:PART, :] = jnp.broadcast_to(sums, (PART - USED, C)).astype(BF)
    keep_ref[...] = held[core]
    send_ref[...] = held[1 - core]


def weight_terms(place, u1, v1, u2, v2):
    shape = jax.ShapeDtypeStruct((PARTS, PART, C), BF)
    return pl.pallas_call(
        weight_kernel,
        out_shape=[shape, shape],
        in_specs=[SMEM] + [VMEM] * 4,
        out_specs=[VMEM] * 2,
        scratch_shapes=[pltpu.VMEM((2, PARTS, PART, C), BF)],
        compiler_params=pltpu.CompilerParams(vmem_limit_bytes=16 << 20),
        cost_estimate=pl.CostEstimate(flops=2 * 10**9, bytes_accessed=4 << 20, transcendentals=0),
        name="weights",
    )(place, u1, v1, u2, v2)


def split_kernel(ways, spot, count, place_ref, *refs):
    owns, arrived, outs, total = refs[:count], refs[count : -1 - ways], refs[-1 - ways : -1], refs[-1]
    pair, _, rows, _ = total.shape
    for index, ref in enumerate(owns):
        value = ref[...].astype(F32)
        for more in arrived:
            value = value + more[...].astype(F32)
        value = value.reshape(pair // count, ways, rows, C)
        total[index * (pair // count) : (index + 1) * (pair // count)] = value
    here = spot(place_ref[0])
    outs[0][...] = total[:, here]
    for step in range(1, ways):
        outs[step][...] = total[:, (here + step) % ways].astype(BF)


def split(place, owns, arrived, pair, rows, ways, spot):
    return pl.pallas_call(
        lambda *refs: split_kernel(ways, spot, len(owns), *refs),
        out_shape=[jax.ShapeDtypeStruct((pair, rows, C), F32)]
        + [jax.ShapeDtypeStruct((pair, rows, C), BF)] * (ways - 1),
        in_specs=[SMEM] + [VMEM] * (len(owns) + len(arrived)),
        out_specs=[VMEM] * ways,
        scratch_shapes=[pltpu.VMEM((pair, ways, rows, C), F32)],
        compiler_params=pltpu.CompilerParams(vmem_limit_bytes=8 << 20),
        name="split",
    )(place, *owns, *arrived)


def join_kernel(ways, spot, place_ref, *refs):
    here = spot(place_ref[0])
    out = refs[-1]
    for step in range(ways):
        out[:, (here - step + ways) % ways] = refs[step][...]


def join(place, pieces, spot):
    ways = len(pieces)
    pair, rows, _ = pieces[0].shape
    joined = pl.pallas_call(
        lambda *refs: join_kernel(ways, spot, *refs),
        out_shape=jax.ShapeDtypeStruct((pair, ways, rows, C), BF),
        in_specs=[SMEM] + [VMEM] * ways,
        out_specs=VMEM,
        compiler_params=pltpu.CompilerParams(vmem_limit_bytes=8 << 20),
        name="join",
    )(place, *pieces)
    return joined.reshape(pair, ways * rows, C)


def sum_kernel(*refs):
    value = refs[0][...]
    for ref in refs[1:-1]:
        value = value + ref[...].astype(F32)
    refs[-1][...] = value.astype(refs[-1].dtype)


def added(dtype, *args):
    return pl.pallas_call(
        sum_kernel,
        out_shape=jax.ShapeDtypeStruct(args[0].shape, dtype),
        in_specs=[VMEM] * len(args),
        out_specs=VMEM,
        compiler_params=pltpu.CompilerParams(vmem_limit_bytes=8 << 20),
        name="added",
    )(*args)


def y_of(place):
    return (place // 2) % 4


def z_high(place):
    return place // 16


def z_low(place):
    return (place // 8) % 2


def core_step(place, step):
    return place ^ 1


def y_step(place, step):
    return (place // 8) * 8 + ((place // 2 + step) % 4) * 2 + place % 2


def z_high_step(place, step):
    return (place + 16 * step) % SPACE


def z_low_step(place, step):
    return place ^ 8


def send(array, move, step):
    return lax.ppermute(array, "space", [(place, move(place, step)) for place in range(SPACE)])


def first_phases(place, terms):
    keep, given = weight_terms(place, *terms)
    arrived = [send(given, core_step, 1)]
    pieces = split(place, [keep], arrived, 1, PART, PARTS, y_of)
    arrived = [send(pieces[step], y_step, step) for step in (2, 1, 3)]
    return added(F32, pieces[0], *arrived)


def last_phases(place, totals):
    pieces = split(place, totals, [], 2, 4 * PIECE, 2, z_low)
    own = added(F32, pieces[0], send(pieces[1], z_low_step, 1))
    pieces = split(place, [own], [], 2, PIECE, 4, z_high)
    arrived = [send(pieces[step], z_high_step, step) for step in (2, 1, 3)]
    whole = added(BF, pieces[0], *arrived)
    moved = {step: send(whole, z_high_step, step) for step in (2, 1, 3)}
    whole = join(place, [whole] + [moved[step] for step in range(1, 4)], z_high)
    own = join_pair(place, [whole, send(whole, z_low_step, 1)])
    behind = [send(part, y_step, 1) for part in own]
    ahead = [send(part, y_step, 3) for part in own]
    across = [send(behind[0], y_step, 1), send(ahead[1], y_step, 3)]
    return [
        join_y(place, [own[half], behind[half], across[half], ahead[half]]) for half in range(2)
    ]


def join_pair_kernel(place_ref, *refs):
    here = z_low(place_ref[0])
    outs = refs[2:]
    for step in range(2):
        for half in range(2):
            outs[half][(here - step + 2) % 2] = refs[step][half]


def join_pair(place, pieces):
    rows = pieces[0].shape[1]
    shape = jax.ShapeDtypeStruct((2, rows, C), BF)
    joined = pl.pallas_call(
        join_pair_kernel,
        out_shape=[shape, shape],
        in_specs=[SMEM] + [VMEM] * 2,
        out_specs=[VMEM] * 2,
        compiler_params=pltpu.CompilerParams(vmem_limit_bytes=8 << 20),
        name="join_pair",
    )(place, *pieces)
    return [part.reshape(2 * rows, C) for part in joined]


def join_y_kernel(place_ref, *refs):
    here = y_of(place_ref[0])
    for step in range(4):
        refs[4][(here - step + 4) % 4] = refs[step][...]


def join_y(place, pieces):
    return pl.pallas_call(
        join_y_kernel,
        out_shape=jax.ShapeDtypeStruct((PARTS, PART, C), BF),
        in_specs=[SMEM] + [VMEM] * 4,
        out_specs=VMEM,
        compiler_params=pltpu.CompilerParams(vmem_limit_bytes=8 << 20),
        name="join_y",
    )(place, *pieces)


def unpack_kernel(place_ref, enc_ref, dec_ref, *refs):
    weight_ref, bias_ref = refs[-2:]

    def write(ref):
        first = 9 * pl.program_id(1)
        for part in range(PARTS):
            rows = slice(part * (C // PARTS), (part + 1) * (C // PARTS))
            for j in range(9):
                row = pl.multiple_of((first + j) * (C // PARTS), C // PARTS)
                weight_ref[0, 0, rows, j * C : (j + 1) * C] = ref[
                    part, pl.ds(row, C // PARTS), :
                ].astype(F32)
        bias_ref[0] = ref[0, USED : USED + 16, :].astype(F32)[0:1]

    encoder = pl.program_id(0) == 0
    pl.when(encoder)(lambda: write(enc_ref))
    pl.when(jnp.logical_not(encoder))(lambda: write(dec_ref))


def unpack(place, flip, parts, onto=()):
    def spot(block, a, place_ref):
        return 2 * block + (place_ref[0] + flip) % 2

    return pl.pallas_call(
        lambda *refs: unpack_kernel(*refs),
        out_shape=[
            jax.ShapeDtypeStruct((4, 3, C, 9 * C), F32),
            jax.ShapeDtypeStruct((4, 1, C), F32),
        ],
        grid_spec=pltpu.PrefetchScalarGridSpec(
            num_scalar_prefetch=1,
            grid=(2, 3),
            in_specs=[VMEM] * 2 + [ANY] * len(onto),
            out_specs=[
                pl.BlockSpec((1, 1, C, 9 * C), lambda *at: (spot(*at), at[1], 0, 0)),
                pl.BlockSpec((1, 1, C), lambda *at: (spot(*at), 0, 0)),
            ],
        ),
        input_output_aliases={3 + index: index for index in range(len(onto))},
        compiler_params=pltpu.CompilerParams(vmem_limit_bytes=16 << 20),
        name="unpack",
    )(place, *parts, *onto)


def to_cells(block):
    return block.transpose(1, 3, 2, 0).reshape(CELLS, W)


def from_cells(field):
    return field.reshape(ROWS, Z, Y, C).transpose(3, 0, 2, 1)[None, None]


def whole_pass(encoder_inputs, upper_inputs, output_cotangent, weights, biases):
    section = lax.axis_index("section")
    space = lax.axis_index("space")
    place = jnp.stack([space, section]).astype(jnp.int32)
    kernels = weights[0]
    bias_rows = jnp.concatenate([biases[0], biases[0]], axis=1)
    enc = to_cells(encoder_inputs[0, 0])
    far_left = beside(enc[CELLS - 2 * Z :], 2)
    far_right = beside(enc[: 2 * Z], -2)
    left = beside(enc, 1)
    right = beside(enc, -1)
    rest = jnp.concatenate([to_cells(upper_inputs[0, 0]), to_cells(output_cotangent[0])], axis=0)
    rest_left = beside(rest, 1)
    rest_right = beside(rest, -1)
    enc_v, enc_h, enc_s1, enc_s2, enc_out = forward(
        encode_kernel, [sds(12, BF)],
        place, kernels, bias_rows, far_left, left, enc, right, far_right,
    )
    dec_v, dec_h, dec_s1, dec_s2 = forward(
        decode_kernel, [],
        place, kernels, bias_rows, enc_out, rest_left, rest, rest_right,
    )
    cot = (
        rest_left[2 * CELLS - 2 * Z :],
        rest[CELLS:],
        rest_right[CELLS : CELLS + 2 * Z],
    )
    slopes = (dec_s1, dec_s2)
    state = tick(2, None, place, kernels, slopes, cot)
    for turn in range(1, SECTIONS):
        cot = hand_on(state, turn - 1, 1)
        state = tick(2, turn, place, kernels, slopes, cot, state=state)
    upper = state
    skip = (beside(upper[4], 1), upper[2], beside(upper[3], -1))
    slopes = (enc_s1, enc_s2)
    state = tick(0, None, place, kernels, slopes, skip)
    for turn in range(SECTIONS - 2, -1, -1):
        cot = hand_on(state, turn + 1, -1)
        if turn == 1:
            dec_total = first_phases(place, (upper[1], dec_v, upper[0], dec_h))
        state = tick(0, turn, place, kernels, slopes, cot, skip=skip, state=state)
    enc_total = first_phases(place, (state[1], enc_v, state[0], enc_h))
    mine = last_phases(place, [enc_total, dec_total])
    other = [send(part, core_step, 1) for part in mine]
    totals = unpack(place, 0, mine)
    weight_total, bias_total = unpack(place, 1, other, totals)
    return (
        from_cells(state[2]),
        from_cells(upper[2]),
        weight_total[None],
        bias_total.reshape(1, 4, C),
    )


def solution(mesh):
    return jax.shard_map(
        whole_pass,
        mesh=mesh,
        in_specs=(
            P("section", None, None, "space", None, None),
            P("section", None, None, "space", None, None),
            P(None, None, "space", None, None),
            P("section", None, None, None, None),
            P("section", None, None),
        ),
        out_specs=(
            P("section", None, None, "space", None, None),
            P("section", None, None, "space", None, None),
            P("section", None, None, None, None),
            P("section", None, None),
        ),
        check_vma=False,
    )
```

```python
import jax
import jax.numpy as jnp
from jax import lax
from jax.experimental import pallas as pl
from jax.experimental.pallas import tpu as pltpu
from jax.sharding import PartitionSpec as P


C = 128
Y = 2
Z = 64
W = Y * C
SPACE = 64
SECTIONS = 4
ROWS = 4
CELLS = ROWS * Z
BF = jnp.bfloat16
F32 = jnp.float32
VMEM = pl.BlockSpec(memory_space=pltpu.VMEM)
ANY = pl.BlockSpec(memory_space=pl.ANY)
SMEM = pl.BlockSpec(memory_space=pltpu.SMEM)


def z_shifts(value):
    count = value.shape[0]
    wide = value.astype(F32)
    depth = lax.broadcasted_iota(jnp.int32, (count, W), 0) % Z
    below = jnp.where(depth == 0, 0.0, pltpu.roll(wide, 1, 0)).astype(BF)
    above = jnp.where(depth == Z - 1, 0.0, pltpu.roll(wide, count - 1, 0)).astype(BF)
    return below, value, above


def tap(w, a, b, c):
    lane = (3 * b + c) * C
    return w[a, :, lane : lane + C]


def row_mask(count, first, place):
    row = lax.broadcasted_iota(jnp.int32, (count * Z, W), 0) // Z + (first + ROWS * place)
    return (row >= 0) & (row < SPACE * ROWS)


def conv(value, w, out_rows):
    stacked = jnp.concatenate(z_shifts(value), axis=1)
    total = None
    for a in range(3):
        kernel = jnp.concatenate(
            [
                jnp.concatenate([tap(w, a, y_in - y_out + 1, c) for c in range(3) for y_in in range(Y)], axis=1)
                for y_out in range(Y)
            ],
            axis=0,
        )
        part = lax.dot_general(
            stacked[a * Z : (a + out_rows) * Z],
            kernel,
            (((1,), (1,)), ((), ())),
            preferred_element_type=F32,
        )
        total = part if total is None else total + part
    return total


def conv_adjoint(value, w, out_rows):
    below, same, above = z_shifts(value)
    stacked = jnp.concatenate([above, same, below], axis=1)
    total = None
    for a in range(3):
        kernel = jnp.concatenate(
            [
                jnp.concatenate([tap(w, a, y_in - y_out + 1, c) for y_in in range(Y)], axis=1)
                for c in range(3)
                for y_out in range(Y)
            ],
            axis=0,
        )
        part = jnp.dot(
            stacked[(2 - a) * Z : (2 - a + out_rows) * Z], kernel, preferred_element_type=F32
        )
        total = part if total is None else total + part
    return total


def gated(pre):
    logistic = jax.nn.sigmoid(pre)
    return pre * logistic, logistic * (1.0 + pre * (1.0 - logistic))


def middle(value, halo, keep):
    return value[(halo - keep) * Z : (halo + ROWS + keep) * Z]


def encode_kernel(place_ref, w_ref, bias_ref, far_left, left, own, right, far_right, *outs):
    v_ref, h_ref, s1_ref, s2_ref, out_ref = outs
    inputs = jnp.concatenate(
        [far_left[...], left[...], own[...], right[...], far_right[...]], axis=0
    )
    v_ref[...] = middle(inputs, 6, 1)
    act, slope = gated(conv(inputs, w_ref.at[0], 14) + bias_ref[0:1, :])
    s1_ref[...] = middle(slope, 5, 1)
    act = jnp.where(row_mask(14, -5, place_ref[0]), act, 0.0).astype(BF)
    h_ref[...] = middle(act, 5, 1)
    act, slope = gated(conv(act, w_ref.at[1], 12) + bias_ref[1:2, :])
    s2_ref[...] = middle(slope, 4, 2)
    out_ref[...] = act.astype(BF)


def decode_kernel(place_ref, w_ref, bias_ref, enc_ref, left, own, right, *outs):
    v_ref, h_ref, s1_ref, s2_ref = outs
    place = place_ref[0]
    upper = jnp.concatenate([left[0:CELLS], own[0:CELLS], right[0:CELLS]], axis=0)
    act = enc_ref[...].astype(F32) + upper.astype(F32)
    act = jnp.where(row_mask(12, -4, place), act, 0.0).astype(BF)
    v_ref[...] = middle(act, 4, 1)
    act, slope = gated(conv(act, w_ref.at[2], 10) + bias_ref[2:3, :])
    s1_ref[...] = middle(slope, 3, 1)
    act = jnp.where(row_mask(10, -3, place), act, 0.0).astype(BF)
    h_ref[...] = middle(act, 3, 1)
    _, slope = gated(conv(act, w_ref.at[3], 8) + bias_ref[3:4, :])
    s2_ref[...] = middle(slope, 2, 2)


def sds(rows, dtype):
    return jax.ShapeDtypeStruct((rows * Z, W), dtype)


def forward(kernel, more, *args):
    return pl.pallas_call(
        kernel,
        out_shape=[sds(6, BF), sds(6, BF), sds(6, F32), sds(8, F32)] + more,
        in_specs=[SMEM] + [VMEM] * (len(args) - 1),
        out_specs=[VMEM] * (4 + len(more)),
        compiler_params=pltpu.CompilerParams(vmem_limit_bytes=16 << 20),
        cost_estimate=pl.CostEstimate(flops=3 * 10**9, bytes_accessed=5 << 20, transcendentals=0),
    )(*args)


def tick_kernel(layer, turn, seeded, place_ref, w_ref, *refs):
    names = list(refs)
    s1_ref, s2_ref = names[0:2]
    cots = [names[2:5]]
    rest = names[5:]
    if seeded == "sum":
        cots.append(rest[0:3])
        rest = rest[3:]
    outs = rest[-5:]
    place = place_ref[0]

    def run():
        def window(three):
            low, mid, high = (ref[...] for ref in three)
            return jnp.concatenate([low, mid, high], axis=0)

        g = window(cots[0]).astype(F32)
        if len(cots) > 1:
            g = (g + window(cots[1]).astype(F32)).astype(BF).astype(F32)
        second = (g * s2_ref[...]).astype(BF)
        outs[0][...] = second[2 * Z : 2 * Z + CELLS]
        first = conv_adjoint(second, w_ref.at[layer + 1], 6) * s1_ref[...]
        first = jnp.where(row_mask(6, -1, place), first, 0.0).astype(BF)
        outs[1][...] = first[Z : Z + CELLS]
        grad = conv_adjoint(first, w_ref.at[layer], 4).astype(BF)
        outs[2][...] = grad
        outs[3][...] = grad[0 : 2 * Z]
        outs[4][...] = grad[CELLS - 2 * Z : CELLS]

    if turn is None:
        run()
        return

    def carry():
        for out, ref in zip(outs, rest[:5]):
            out[...] = ref[...]

    mine = place_ref[1] == turn
    pl.when(mine)(run)
    pl.when(jnp.logical_not(mine))(carry)


def tick(layer, turn, place, weights, slopes, cot, skip=None, state=None):
    args = [place, weights, *slopes, *cot]
    seeded = "plain"
    if skip is not None:
        args += list(skip)
        seeded = "sum"
    if state is not None:
        args += list(state)
    return pl.pallas_call(
        lambda *refs: tick_kernel(layer, turn, seeded, *refs),
        out_shape=[sds(4, BF)] * 3 + [sds(2, BF)] * 2,
        in_specs=[SMEM] + [VMEM] * (len(args) - 1),
        out_specs=[VMEM] * 5,
        compiler_params=pltpu.CompilerParams(vmem_limit_bytes=16 << 20),
        cost_estimate=pl.CostEstimate(flops=3 * 10**9, bytes_accessed=4 << 20, transcendentals=0),
        name="tick",
    )(*args)


PARTS = 4
PIECES = 8
USED = 27 * C // PARTS
PIECE = 112
PART = PIECES * PIECE
GRID_AXES = ("section", "space")


def shifted(source_section, by, step):
    pairs = []
    for place in range(SPACE):
        if 0 <= place + step < SPACE:
            source = source_section * SPACE + place
            pairs.append((source, source + by * SPACE + step))
    return pairs


def hand_on(state, source_section, by):
    grad, low, high = state[2:5]
    middle = lax.ppermute(grad, GRID_AXES, shifted(source_section, by, 0))
    before = lax.ppermute(high, GRID_AXES, shifted(source_section, by, 1))
    after = lax.ppermute(low, GRID_AXES, shifted(source_section, by, -1))
    return (before, middle, after)


def beside(array, step):
    pairs = [(place, place + step) for place in range(SPACE) if 0 <= place + step < SPACE]
    return lax.ppermute(array, "space", pairs)


def weight_kernel(place_ref, u1_ref, v1_ref, u2_ref, v2_ref, keep_ref, send_ref, held):
    core = place_ref[0] % 2
    for layer, (u_ref, v_ref) in enumerate(((u1_ref, v1_ref), (u2_ref, v2_ref))):
        grads = u_ref[...]
        wide = grads.astype(F32)
        turned = wide.T.astype(BF)
        stacked = jnp.concatenate(z_shifts(v_ref[...]), axis=1)
        for a in range(3):
            product = jnp.dot(
                turned, stacked[a * Z : a * Z + CELLS], preferred_element_type=F32
            )

            def block(y_out, c, y_in):
                lane = (c * Y + y_in) * C
                return product[y_out * C : (y_out + 1) * C, lane : lane + C]

            for c in range(3):
                blocks = (block(1, c, 0), block(0, c, 0) + block(1, c, 1), block(0, c, 1))
                for b in range(3):
                    value = blocks[b].astype(BF)
                    row = (9 * a + 3 * b + c) * (C // PARTS)
                    for part in range(PARTS):
                        held[layer, part, row : row + C // PARTS, :] = value[
                            part * (C // PARTS) : (part + 1) * (C // PARTS)
                        ]
        sums = jnp.sum(wide, axis=0, keepdims=True)
        sums = sums[:, 0:C] + sums[:, C : 2 * C]
        for part in range(PARTS):
            held[layer, part, USED:PART, :] = jnp.broadcast_to(sums, (PART - USED, C)).astype(BF)
    keep_ref[...] = held[core]
    send_ref[...] = held[1 - core]


def weight_terms(place, u1, v1, u2, v2):
    shape = jax.ShapeDtypeStruct((PARTS, PART, C), BF)
    return pl.pallas_call(
        weight_kernel,
        out_shape=[shape, shape],
        in_specs=[SMEM] + [VMEM] * 4,
        out_specs=[VMEM] * 2,
        scratch_shapes=[pltpu.VMEM((2, PARTS, PART, C), BF)],
        compiler_params=pltpu.CompilerParams(vmem_limit_bytes=16 << 20),
        cost_estimate=pl.CostEstimate(flops=2 * 10**9, bytes_accessed=4 << 20, transcendentals=0),
        name="weights",
    )(place, u1, v1, u2, v2)


def split_kernel(ways, spot, count, place_ref, *refs):
    owns, arrived, outs, total = refs[:count], refs[count : -1 - ways], refs[-1 - ways : -1], refs[-1]
    pair, _, rows, _ = total.shape
    for index, ref in enumerate(owns):
        value = ref[...].astype(F32)
        for more in arrived:
            value = value + more[...].astype(F32)
        value = value.reshape(pair // count, ways, rows, C)
        total[index * (pair // count) : (index + 1) * (pair // count)] = value
    here = spot(place_ref[0])
    outs[0][...] = total[:, here]
    for step in range(1, ways):
        outs[step][...] = total[:, (here + step) % ways].astype(BF)


def split(place, owns, arrived, pair, rows, ways, spot):
    return pl.pallas_call(
        lambda *refs: split_kernel(ways, spot, len(owns), *refs),
        out_shape=[jax.ShapeDtypeStruct((pair, rows, C), F32)]
        + [jax.ShapeDtypeStruct((pair, rows, C), BF)] * (ways - 1),
        in_specs=[SMEM] + [VMEM] * (len(owns) + len(arrived)),
        out_specs=[VMEM] * ways,
        scratch_shapes=[pltpu.VMEM((pair, ways, rows, C), F32)],
        compiler_params=pltpu.CompilerParams(vmem_limit_bytes=8 << 20),
        name="split",
    )(place, *owns, *arrived)


def join_kernel(ways, spot, place_ref, *refs):
    here = spot(place_ref[0])
    out = refs[-1]
    for step in range(ways):
        out[:, (here - step + ways) % ways] = refs[step][...]


def join(place, pieces, spot):
    ways = len(pieces)
    pair, rows, _ = pieces[0].shape
    joined = pl.pallas_call(
        lambda *refs: join_kernel(ways, spot, *refs),
        out_shape=jax.ShapeDtypeStruct((pair, ways, rows, C), BF),
        in_specs=[SMEM] + [VMEM] * ways,
        out_specs=VMEM,
        compiler_params=pltpu.CompilerParams(vmem_limit_bytes=8 << 20),
        name="join",
    )(place, *pieces)
    return joined.reshape(pair, ways * rows, C)


def sum_kernel(*refs):
    value = refs[0][...]
    for ref in refs[1:-1]:
        value = value + ref[...].astype(F32)
    refs[-1][...] = value.astype(refs[-1].dtype)


def added(dtype, *args):
    return pl.pallas_call(
        sum_kernel,
        out_shape=jax.ShapeDtypeStruct(args[0].shape, dtype),
        in_specs=[VMEM] * len(args),
        out_specs=VMEM,
        compiler_params=pltpu.CompilerParams(vmem_limit_bytes=8 << 20),
        name="added",
    )(*args)


def y_of(place):
    return (place // 2) % 4


def z_high(place):
    return place // 16


def z_low(place):
    return (place // 8) % 2


def core_step(place, step):
    return place ^ 1


def y_step(place, step):
    return (place // 8) * 8 + ((place // 2 + step) % 4) * 2 + place % 2


def z_high_step(place, step):
    return (place + 16 * step) % SPACE


def z_low_step(place, step):
    return place ^ 8


def send(array, move, step):
    return lax.ppermute(array, "space", [(place, move(place, step)) for place in range(SPACE)])


def first_phases(place, terms):
    keep, given = weight_terms(place, *terms)
    arrived = [send(given, core_step, 1)]
    pieces = split(place, [keep], arrived, 1, PART, PARTS, y_of)
    arrived = [send(pieces[step], y_step, step) for step in (2, 1, 3)]
    return added(F32, pieces[0], *arrived)


def last_phases(place, totals):
    pieces = split(place, totals, [], 2, 4 * PIECE, 2, z_low)
    own = added(F32, pieces[0], send(pieces[1], z_low_step, 1))
    pieces = split(place, [own], [], 2, PIECE, 4, z_high)
    arrived = [send(pieces[step], z_high_step, step) for step in (2, 1, 3)]
    whole = added(BF, pieces[0], *arrived)
    moved = {step: send(whole, z_high_step, step) for step in (2, 1, 3)}
    whole = join(place, [whole] + [moved[step] for step in range(1, 4)], z_high)
    own = join_pair(place, [whole, send(whole, z_low_step, 1)])
    behind = [send(part, y_step, 1) for part in own]
    ahead = [send(part, y_step, 3) for part in own]
    across = [send(behind[0], y_step, 1), send(ahead[1], y_step, 3)]
    return [
        join_y(place, [own[half], behind[half], across[half], ahead[half]]) for half in range(2)
    ]


def join_pair_kernel(place_ref, *refs):
    here = z_low(place_ref[0])
    outs = refs[2:]
    for step in range(2):
        for half in range(2):
            outs[half][(here - step + 2) % 2] = refs[step][half]


def join_pair(place, pieces):
    rows = pieces[0].shape[1]
    shape = jax.ShapeDtypeStruct((2, rows, C), BF)
    joined = pl.pallas_call(
        join_pair_kernel,
        out_shape=[shape, shape],
        in_specs=[SMEM] + [VMEM] * 2,
        out_specs=[VMEM] * 2,
        compiler_params=pltpu.CompilerParams(vmem_limit_bytes=8 << 20),
        name="join_pair",
    )(place, *pieces)
    return [part.reshape(2 * rows, C) for part in joined]


def join_y_kernel(place_ref, *refs):
    here = y_of(place_ref[0])
    for step in range(4):
        refs[4][(here - step + 4) % 4] = refs[step][...]


def join_y(place, pieces):
    return pl.pallas_call(
        join_y_kernel,
        out_shape=jax.ShapeDtypeStruct((PARTS, PART, C), BF),
        in_specs=[SMEM] + [VMEM] * 4,
        out_specs=VMEM,
        compiler_params=pltpu.CompilerParams(vmem_limit_bytes=8 << 20),
        name="join_y",
    )(place, *pieces)


def unpack_kernel(place_ref, enc_ref, dec_ref, *refs):
    weight_ref, bias_ref = refs[-2:]

    def write(ref):
        def one(index, carry):
            part, a = index // 3, index % 3
            rows = pl.ds(pl.multiple_of(part * (C // PARTS), C // PARTS), C // PARTS)
            for j in range(9):
                row = pl.multiple_of((9 * a + j) * (C // PARTS), C // PARTS)
                weight_ref[0, a, rows, j * C : (j + 1) * C] = ref[
                    part, pl.ds(row, C // PARTS), :
                ].astype(F32)
            return carry

        lax.fori_loop(0, 3 * PARTS, one, 0)
        bias_ref[0] = ref[0, USED : USED + 16, :].astype(F32)[0:1]

    encoder = pl.program_id(0) == 0
    pl.when(encoder)(lambda: write(enc_ref))
    pl.when(jnp.logical_not(encoder))(lambda: write(dec_ref))


def unpack(place, flip, parts, onto=()):
    def spot(block, place_ref):
        return 2 * block + (place_ref[0] + flip) % 2

    return pl.pallas_call(
        lambda *refs: unpack_kernel(*refs),
        out_shape=[
            jax.ShapeDtypeStruct((4, 3, C, 9 * C), F32),
            jax.ShapeDtypeStruct((4, 1, C), F32),
        ],
        grid_spec=pltpu.PrefetchScalarGridSpec(
            num_scalar_prefetch=1,
            grid=(2,),
            in_specs=[VMEM] * 2 + [ANY] * len(onto),
            out_specs=[
                pl.BlockSpec((1, 3, C, 9 * C), lambda *at: (spot(*at), 0, 0, 0)),
                pl.BlockSpec((1, 1, C), lambda *at: (spot(*at), 0, 0)),
            ],
        ),
        input_output_aliases={3 + index: index for index in range(len(onto))},
        compiler_params=pltpu.CompilerParams(vmem_limit_bytes=16 << 20),
        name="unpack",
    )(place, *parts, *onto)


def to_cells(block):
    return block.transpose(1, 3, 2, 0).reshape(CELLS, W)


def from_cells(field):
    return field.reshape(ROWS, Z, Y, C).transpose(3, 0, 2, 1)[None, None]


def whole_pass(encoder_inputs, upper_inputs, output_cotangent, weights, biases):
    section = lax.axis_index("section")
    space = lax.axis_index("space")
    place = jnp.stack([space, section]).astype(jnp.int32)
    kernels = weights[0]
    bias_rows = jnp.concatenate([biases[0], biases[0]], axis=1)
    enc = to_cells(encoder_inputs[0, 0])
    far_left = beside(enc[CELLS - 2 * Z :], 2)
    far_right = beside(enc[: 2 * Z], -2)
    left = beside(enc, 1)
    right = beside(enc, -1)
    rest = jnp.concatenate([to_cells(upper_inputs[0, 0]), to_cells(output_cotangent[0])], axis=0)
    rest_left = beside(rest, 1)
    rest_right = beside(rest, -1)
    enc_v, enc_h, enc_s1, enc_s2, enc_out = forward(
        encode_kernel, [sds(12, BF)],
        place, kernels, bias_rows, far_left, left, enc, right, far_right,
    )
    dec_v, dec_h, dec_s1, dec_s2 = forward(
        decode_kernel, [],
        place, kernels, bias_rows, enc_out, rest_left, rest, rest_right,
    )
    cot = (
        rest_left[2 * CELLS - 2 * Z :],
        rest[CELLS:],
        rest_right[CELLS : CELLS + 2 * Z],
    )
    slopes = (dec_s1, dec_s2)
    state = tick(2, None, place, kernels, slopes, cot)
    for turn in range(1, SECTIONS):
        cot = hand_on(state, turn - 1, 1)
        state = tick(2, turn, place, kernels, slopes, cot, state=state)
    upper = state
    skip = (beside(upper[4], 1), upper[2], beside(upper[3], -1))
    slopes = (enc_s1, enc_s2)
    state = tick(0, None, place, kernels, slopes, skip)
    for turn in range(SECTIONS - 2, -1, -1):
        cot = hand_on(state, turn + 1, -1)
        if turn == 1:
            dec_total = first_phases(place, (upper[1], dec_v, upper[0], dec_h))
        state = tick(0, turn, place, kernels, slopes, cot, skip=skip, state=state)
    enc_total = first_phases(place, (state[1], enc_v, state[0], enc_h))
    encoder_grad, upper_grad = from_cells(state[2]), from_cells(upper[2])
    mine = last_phases(place, [enc_total, dec_total])
    other = [send(part, core_step, 1) for part in mine]
    totals = unpack(place, 0, mine)
    weight_total, bias_total = unpack(place, 1, other, totals)
    return (
        encoder_grad,
        upper_grad,
        weight_total[None],
        bias_total.reshape(1, 4, C),
    )


def solution(mesh):
    return jax.shard_map(
        whole_pass,
        mesh=mesh,
        in_specs=(
            P("section", None, None, "space", None, None),
            P("section", None, None, "space", None, None),
            P(None, None, "space", None, None),
            P("section", None, None, None, None),
            P("section", None, None),
        ),
        out_specs=(
            P("section", None, None, "space", None, None),
            P("section", None, None, "space", None, None),
            P("section", None, None, None, None),
            P("section", None, None),
        ),
        check_vma=False,
    )
```

```python
import jax
import jax.numpy as jnp
from jax import lax
from jax.experimental import pallas as pl
from jax.experimental.pallas import tpu as pltpu
from jax.sharding import PartitionSpec as P


C = 128
Y = 2
Z = 64
W = Y * C
SPACE = 64
SECTIONS = 4
ROWS = 4
CELLS = ROWS * Z
BF = jnp.bfloat16
F32 = jnp.float32
VMEM = pl.BlockSpec(memory_space=pltpu.VMEM)
ANY = pl.BlockSpec(memory_space=pl.ANY)
SMEM = pl.BlockSpec(memory_space=pltpu.SMEM)


def z_shifts(value):
    count = value.shape[0]
    wide = value.astype(F32)
    depth = lax.broadcasted_iota(jnp.int32, (count, W), 0) % Z
    below = jnp.where(depth == 0, 0.0, pltpu.roll(wide, 1, 0)).astype(BF)
    above = jnp.where(depth == Z - 1, 0.0, pltpu.roll(wide, count - 1, 0)).astype(BF)
    return below, value, above


def tap(w, a, b, c):
    lane = (3 * b + c) * C
    return w[a, :, lane : lane + C]


def row_mask(count, first, place):
    row = lax.broadcasted_iota(jnp.int32, (count * Z, W), 0) // Z + (first + ROWS * place)
    return (row >= 0) & (row < SPACE * ROWS)


def conv(value, w, out_rows):
    stacked = jnp.concatenate(z_shifts(value), axis=1)
    total = None
    for a in range(3):
        kernel = jnp.concatenate(
            [
                jnp.concatenate([tap(w, a, y_in - y_out + 1, c) for c in range(3) for y_in in range(Y)], axis=1)
                for y_out in range(Y)
            ],
            axis=0,
        )
        part = lax.dot_general(
            stacked[a * Z : (a + out_rows) * Z],
            kernel,
            (((1,), (1,)), ((), ())),
            preferred_element_type=F32,
        )
        total = part if total is None else total + part
    return total


def conv_adjoint(value, w, out_rows):
    below, same, above = z_shifts(value)
    stacked = jnp.concatenate([above, same, below], axis=1)
    total = None
    for a in range(3):
        kernel = jnp.concatenate(
            [
                jnp.concatenate([tap(w, a, y_in - y_out + 1, c) for y_in in range(Y)], axis=1)
                for c in range(3)
                for y_out in range(Y)
            ],
            axis=0,
        )
        part = jnp.dot(
            stacked[(2 - a) * Z : (2 - a + out_rows) * Z], kernel, preferred_element_type=F32
        )
        total = part if total is None else total + part
    return total


def gated(pre):
    logistic = jax.nn.sigmoid(pre)
    return pre * logistic, logistic * (1.0 + pre * (1.0 - logistic))


def middle(value, halo, keep):
    return value[(halo - keep) * Z : (halo + ROWS + keep) * Z]


def encode_kernel(place_ref, w_ref, bias_ref, far_left, left, own, right, far_right, *outs):
    v_ref, h_ref, s1_ref, s2_ref, out_ref = outs
    inputs = jnp.concatenate(
        [far_left[...], left[...], own[...], right[...], far_right[...]], axis=0
    )
    v_ref[...] = middle(inputs, 6, 1)
    act, slope = gated(conv(inputs, w_ref.at[0], 14) + bias_ref[0:1, :])
    s1_ref[...] = middle(slope, 5, 1)
    act = jnp.where(row_mask(14, -5, place_ref[0]), act, 0.0).astype(BF)
    h_ref[...] = middle(act, 5, 1)
    act, slope = gated(conv(act, w_ref.at[1], 12) + bias_ref[1:2, :])
    s2_ref[...] = middle(slope, 4, 2)
    out_ref[...] = act.astype(BF)


def decode_kernel(place_ref, w_ref, bias_ref, enc_ref, left, own, right, *outs):
    v_ref, h_ref, s1_ref, s2_ref = outs
    place = place_ref[0]
    upper = jnp.concatenate([left[0:CELLS], own[0:CELLS], right[0:CELLS]], axis=0)
    act = enc_ref[...].astype(F32) + upper.astype(F32)
    act = jnp.where(row_mask(12, -4, place), act, 0.0).astype(BF)
    v_ref[...] = middle(act, 4, 1)
    act, slope = gated(conv(act, w_ref.at[2], 10) + bias_ref[2:3, :])
    s1_ref[...] = middle(slope, 3, 1)
    act = jnp.where(row_mask(10, -3, place), act, 0.0).astype(BF)
    h_ref[...] = middle(act, 3, 1)
    _, slope = gated(conv(act, w_ref.at[3], 8) + bias_ref[3:4, :])
    s2_ref[...] = middle(slope, 2, 2)


def sds(rows, dtype):
    return jax.ShapeDtypeStruct((rows * Z, W), dtype)


def forward(kernel, more, *args):
    return pl.pallas_call(
        kernel,
        out_shape=[sds(6, BF), sds(6, BF), sds(6, F32), sds(8, F32)] + more,
        in_specs=[SMEM] + [VMEM] * (len(args) - 1),
        out_specs=[VMEM] * (4 + len(more)),
        compiler_params=pltpu.CompilerParams(vmem_limit_bytes=16 << 20),
        cost_estimate=pl.CostEstimate(flops=3 * 10**9, bytes_accessed=5 << 20, transcendentals=0),
    )(*args)


def tick_kernel(layer, turn, seeded, place_ref, w_ref, *refs):
    names = list(refs)
    s1_ref, s2_ref = names[0:2]
    cots = [names[2:5]]
    rest = names[5:]
    if seeded == "sum":
        cots.append(rest[0:3])
        rest = rest[3:]
    outs = rest[-5:]
    place = place_ref[0]

    def run():
        def window(three):
            low, mid, high = (ref[...] for ref in three)
            return jnp.concatenate([low, mid, high], axis=0)

        g = window(cots[0]).astype(F32)
        if len(cots) > 1:
            g = (g + window(cots[1]).astype(F32)).astype(BF).astype(F32)
        second = (g * s2_ref[...]).astype(BF)
        outs[0][...] = second[2 * Z : 2 * Z + CELLS]
        first = conv_adjoint(second, w_ref.at[layer + 1], 6) * s1_ref[...]
        first = jnp.where(row_mask(6, -1, place), first, 0.0).astype(BF)
        outs[1][...] = first[Z : Z + CELLS]
        grad = conv_adjoint(first, w_ref.at[layer], 4).astype(BF)
        outs[2][...] = grad
        outs[3][...] = grad[0 : 2 * Z]
        outs[4][...] = grad[CELLS - 2 * Z : CELLS]

    if turn is None:
        run()
        return

    def carry():
        for out, ref in zip(outs, rest[:5]):
            out[...] = ref[...]

    mine = place_ref[1] == turn
    pl.when(mine)(run)
    pl.when(jnp.logical_not(mine))(carry)


def final_kernel(place_ref, w_ref, s1_ref, s2_ref, *refs):
    cots, skips, state, outs = refs[0:3], refs[3:6], refs[6:8], refs[8:11]
    mine = place_ref[1] == 0

    @pl.when(mine)
    def _():
        g = jnp.concatenate([ref[...] for ref in cots], axis=0).astype(F32)
        g = g + jnp.concatenate([ref[...] for ref in skips], axis=0).astype(F32)
        second = (g.astype(BF).astype(F32) * s2_ref[...]).astype(BF)
        outs[0][...] = second[2 * Z : 2 * Z + CELLS]
        first = conv_adjoint(second, w_ref.at[1], 6) * s1_ref[...]
        first = jnp.where(row_mask(6, -1, place_ref[0]), first, 0.0).astype(BF)
        outs[1][...] = first[Z : Z + CELLS]
        outs[2][...] = first

    @pl.when(jnp.logical_not(mine))
    def _():
        outs[0][...] = state[0][...]
        outs[1][...] = state[1][...]
        outs[2][...] = jnp.zeros_like(outs[2])


def final_tick(place, weights, slopes, cot, skip, state):
    args = [place, weights, *slopes, *cot, *skip, *state[0:2]]
    return pl.pallas_call(
        final_kernel,
        out_shape=[sds(4, BF), sds(4, BF), sds(6, BF)],
        in_specs=[SMEM] + [VMEM] * (len(args) - 1),
        out_specs=[VMEM] * 3,
        compiler_params=pltpu.CompilerParams(vmem_limit_bytes=16 << 20),
        cost_estimate=pl.CostEstimate(flops=2 * 10**9, bytes_accessed=4 << 20, transcendentals=0),
        name="final_tick",
    )(*args)


def late_kernel(place_ref, w_ref, first_ref, state_ref, out_ref):
    mine = place_ref[1] == 0

    @pl.when(mine)
    def _():
        out_ref[...] = conv_adjoint(first_ref[...], w_ref.at[0], 4).astype(BF)

    @pl.when(jnp.logical_not(mine))
    def _():
        out_ref[...] = state_ref[...]


def late_input_grad(place, weights, first, grad):
    return pl.pallas_call(
        late_kernel,
        out_shape=sds(4, BF),
        in_specs=[SMEM] + [VMEM] * 3,
        out_specs=VMEM,
        compiler_params=pltpu.CompilerParams(vmem_limit_bytes=16 << 20),
        cost_estimate=pl.CostEstimate(flops=10**9, bytes_accessed=2 << 20, transcendentals=0),
        name="late",
    )(place, weights, first, grad)


def tick(layer, turn, place, weights, slopes, cot, skip=None, state=None):
    args = [place, weights, *slopes, *cot]
    seeded = "plain"
    if skip is not None:
        args += list(skip)
        seeded = "sum"
    if state is not None:
        args += list(state)
    return pl.pallas_call(
        lambda *refs: tick_kernel(layer, turn, seeded, *refs),
        out_shape=[sds(4, BF)] * 3 + [sds(2, BF)] * 2,
        in_specs=[SMEM] + [VMEM] * (len(args) - 1),
        out_specs=[VMEM] * 5,
        compiler_params=pltpu.CompilerParams(vmem_limit_bytes=16 << 20),
        cost_estimate=pl.CostEstimate(flops=3 * 10**9, bytes_accessed=4 << 20, transcendentals=0),
        name="tick",
    )(*args)


PARTS = 4
PIECES = 8
USED = 27 * C // PARTS
PIECE = 112
PART = PIECES * PIECE
GRID_AXES = ("section", "space")


def shifted(source_section, by, step):
    pairs = []
    for place in range(SPACE):
        if 0 <= place + step < SPACE:
            source = source_section * SPACE + place
            pairs.append((source, source + by * SPACE + step))
    return pairs


def hand_on(state, source_section, by):
    grad, low, high = state[2:5]
    middle = lax.ppermute(grad, GRID_AXES, shifted(source_section, by, 0))
    before = lax.ppermute(high, GRID_AXES, shifted(source_section, by, 1))
    after = lax.ppermute(low, GRID_AXES, shifted(source_section, by, -1))
    return (before, middle, after)


def beside(array, step):
    pairs = [(place, place + step) for place in range(SPACE) if 0 <= place + step < SPACE]
    return lax.ppermute(array, "space", pairs)


def weight_kernel(place_ref, u1_ref, v1_ref, u2_ref, v2_ref, keep_ref, send_ref, held):
    core = place_ref[0] % 2
    for layer, (u_ref, v_ref) in enumerate(((u1_ref, v1_ref), (u2_ref, v2_ref))):
        grads = u_ref[...]
        wide = grads.astype(F32)
        turned = wide.T.astype(BF)
        stacked = jnp.concatenate(z_shifts(v_ref[...]), axis=1)
        for a in range(3):
            product = jnp.dot(
                turned, stacked[a * Z : a * Z + CELLS], preferred_element_type=F32
            )

            def block(y_out, c, y_in):
                lane = (c * Y + y_in) * C
                return product[y_out * C : (y_out + 1) * C, lane : lane + C]

            for c in range(3):
                blocks = (block(1, c, 0), block(0, c, 0) + block(1, c, 1), block(0, c, 1))
                for b in range(3):
                    value = blocks[b].astype(BF)
                    row = (9 * a + 3 * b + c) * (C // PARTS)
                    for part in range(PARTS):
                        held[layer, part, row : row + C // PARTS, :] = value[
                            part * (C // PARTS) : (part + 1) * (C // PARTS)
                        ]
        sums = jnp.sum(wide, axis=0, keepdims=True)
        sums = sums[:, 0:C] + sums[:, C : 2 * C]
        for part in range(PARTS):
            held[layer, part, USED:PART, :] = jnp.broadcast_to(sums, (PART - USED, C)).astype(BF)
    keep_ref[...] = held[core]
    send_ref[...] = held[1 - core]


def weight_terms(place, u1, v1, u2, v2):
    shape = jax.ShapeDtypeStruct((PARTS, PART, C), BF)
    return pl.pallas_call(
        weight_kernel,
        out_shape=[shape, shape],
        in_specs=[SMEM] + [VMEM] * 4,
        out_specs=[VMEM] * 2,
        scratch_shapes=[pltpu.VMEM((2, PARTS, PART, C), BF)],
        compiler_params=pltpu.CompilerParams(vmem_limit_bytes=16 << 20),
        cost_estimate=pl.CostEstimate(flops=2 * 10**9, bytes_accessed=4 << 20, transcendentals=0),
        name="weights",
    )(place, u1, v1, u2, v2)


def split_kernel(ways, spot, count, place_ref, *refs):
    owns, arrived, outs, total = refs[:count], refs[count : -1 - ways], refs[-1 - ways : -1], refs[-1]
    pair, _, rows, _ = total.shape
    for index, ref in enumerate(owns):
        value = ref[...].astype(F32)
        for more in arrived:
            value = value + more[...].astype(F32)
        value = value.reshape(pair // count, ways, rows, C)
        total[index * (pair // count) : (index + 1) * (pair // count)] = value
    here = spot(place_ref[0])
    outs[0][...] = total[:, here]
    for step in range(1, ways):
        outs[step][...] = total[:, (here + step) % ways].astype(BF)


def split(place, owns, arrived, pair, rows, ways, spot):
    return pl.pallas_call(
        lambda *refs: split_kernel(ways, spot, len(owns), *refs),
        out_shape=[jax.ShapeDtypeStruct((pair, rows, C), F32)]
        + [jax.ShapeDtypeStruct((pair, rows, C), BF)] * (ways - 1),
        in_specs=[SMEM] + [VMEM] * (len(owns) + len(arrived)),
        out_specs=[VMEM] * ways,
        scratch_shapes=[pltpu.VMEM((pair, ways, rows, C), F32)],
        compiler_params=pltpu.CompilerParams(vmem_limit_bytes=8 << 20),
        name="split",
    )(place, *owns, *arrived)


def join_kernel(ways, spot, place_ref, *refs):
    here = spot(place_ref[0])
    out = refs[-1]
    for step in range(ways):
        out[:, (here - step + ways) % ways] = refs[step][...]


def join(place, pieces, spot):
    ways = len(pieces)
    pair, rows, _ = pieces[0].shape
    joined = pl.pallas_call(
        lambda *refs: join_kernel(ways, spot, *refs),
        out_shape=jax.ShapeDtypeStruct((pair, ways, rows, C), BF),
        in_specs=[SMEM] + [VMEM] * ways,
        out_specs=VMEM,
        compiler_params=pltpu.CompilerParams(vmem_limit_bytes=8 << 20),
        name="join",
    )(place, *pieces)
    return joined.reshape(pair, ways * rows, C)


def sum_kernel(*refs):
    value = refs[0][...]
    for ref in refs[1:-1]:
        value = value + ref[...].astype(F32)
    refs[-1][...] = value.astype(refs[-1].dtype)


def added(dtype, *args):
    return pl.pallas_call(
        sum_kernel,
        out_shape=jax.ShapeDtypeStruct(args[0].shape, dtype),
        in_specs=[VMEM] * len(args),
        out_specs=VMEM,
        compiler_params=pltpu.CompilerParams(vmem_limit_bytes=8 << 20),
        name="added",
    )(*args)


def y_of(place):
    return (place // 2) % 4


def z_high(place):
    return place // 16


def z_low(place):
    return (place // 8) % 2


def core_step(place, step):
    return place ^ 1


def y_step(place, step):
    return (place // 8) * 8 + ((place // 2 + step) % 4) * 2 + place % 2


def z_high_step(place, step):
    return (place + 16 * step) % SPACE


def z_low_step(place, step):
    return place ^ 8


def send(array, move, step):
    return lax.ppermute(array, "space", [(place, move(place, step)) for place in range(SPACE)])


def first_phases(place, terms):
    keep, given = weight_terms(place, *terms)
    arrived = [send(given, core_step, 1)]
    pieces = split(place, [keep], arrived, 1, PART, PARTS, y_of)
    arrived = [send(pieces[step], y_step, step) for step in (2, 1, 3)]
    return added(F32, pieces[0], *arrived)


def last_phases(place, totals):
    pieces = split(place, totals, [], 2, 4 * PIECE, 2, z_low)
    own = added(F32, pieces[0], send(pieces[1], z_low_step, 1))
    pieces = split(place, [own], [], 2, PIECE, 4, z_high)
    arrived = [send(pieces[step], z_high_step, step) for step in (2, 1, 3)]
    whole = added(BF, pieces[0], *arrived)
    moved = {step: send(whole, z_high_step, step) for step in (2, 1, 3)}
    whole = join(place, [whole] + [moved[step] for step in range(1, 4)], z_high)
    own = join_pair(place, [whole, send(whole, z_low_step, 1)])
    behind = [send(part, y_step, 1) for part in own]
    ahead = [send(part, y_step, 3) for part in own]
    across = [send(behind[0], y_step, 1), send(ahead[1], y_step, 3)]
    return [
        join_y(place, [own[half], behind[half], across[half], ahead[half]]) for half in range(2)
    ]


def join_pair_kernel(place_ref, *refs):
    here = z_low(place_ref[0])
    outs = refs[2:]
    for step in range(2):
        for half in range(2):
            outs[half][(here - step + 2) % 2] = refs[step][half]


def join_pair(place, pieces):
    rows = pieces[0].shape[1]
    shape = jax.ShapeDtypeStruct((2, rows, C), BF)
    joined = pl.pallas_call(
        join_pair_kernel,
        out_shape=[shape, shape],
        in_specs=[SMEM] + [VMEM] * 2,
        out_specs=[VMEM] * 2,
        compiler_params=pltpu.CompilerParams(vmem_limit_bytes=8 << 20),
        name="join_pair",
    )(place, *pieces)
    return [part.reshape(2 * rows, C) for part in joined]


def join_y_kernel(place_ref, *refs):
    here = y_of(place_ref[0])
    for step in range(4):
        refs[4][(here - step + 4) % 4] = refs[step][...]


def join_y(place, pieces):
    return pl.pallas_call(
        join_y_kernel,
        out_shape=jax.ShapeDtypeStruct((PARTS, PART, C), BF),
        in_specs=[SMEM] + [VMEM] * 4,
        out_specs=VMEM,
        compiler_params=pltpu.CompilerParams(vmem_limit_bytes=8 << 20),
        name="join_y",
    )(place, *pieces)


def unpack_kernel(place_ref, enc_ref, dec_ref, *refs):
    weight_ref, bias_ref = refs[-2:]

    def write(ref):
        def one(index, carry):
            part, a = index // 3, index % 3
            rows = pl.ds(pl.multiple_of(part * (C // PARTS), C // PARTS), C // PARTS)
            for j in range(9):
                row = pl.multiple_of((9 * a + j) * (C // PARTS), C // PARTS)
                weight_ref[0, a, rows, j * C : (j + 1) * C] = ref[
                    part, pl.ds(row, C // PARTS), :
                ].astype(F32)
            return carry

        lax.fori_loop(0, 3 * PARTS, one, 0)
        bias_ref[0] = ref[0, USED : USED + 16, :].astype(F32)[0:1]

    encoder = pl.program_id(0) == 0
    pl.when(encoder)(lambda: write(enc_ref))
    pl.when(jnp.logical_not(encoder))(lambda: write(dec_ref))


def unpack(place, flip, parts, onto=()):
    def spot(block, place_ref):
        return 2 * block + (place_ref[0] + flip) % 2

    return pl.pallas_call(
        lambda *refs: unpack_kernel(*refs),
        out_shape=[
            jax.ShapeDtypeStruct((4, 3, C, 9 * C), F32),
            jax.ShapeDtypeStruct((4, 1, C), F32),
        ],
        grid_spec=pltpu.PrefetchScalarGridSpec(
            num_scalar_prefetch=1,
            grid=(2,),
            in_specs=[VMEM] * 2 + [ANY] * len(onto),
            out_specs=[
                pl.BlockSpec((1, 3, C, 9 * C), lambda *at: (spot(*at), 0, 0, 0)),
                pl.BlockSpec((1, 1, C), lambda *at: (spot(*at), 0, 0)),
            ],
        ),
        input_output_aliases={3 + index: index for index in range(len(onto))},
        compiler_params=pltpu.CompilerParams(vmem_limit_bytes=16 << 20),
        name="unpack",
    )(place, *parts, *onto)


def to_cells(block):
    return block.transpose(1, 3, 2, 0).reshape(CELLS, W)


def from_cells(field):
    return field.reshape(ROWS, Z, Y, C).transpose(3, 0, 2, 1)[None, None]


def whole_pass(encoder_inputs, upper_inputs, output_cotangent, weights, biases):
    section = lax.axis_index("section")
    space = lax.axis_index("space")
    place = jnp.stack([space, section]).astype(jnp.int32)
    kernels = weights[0]
    bias_rows = jnp.concatenate([biases[0], biases[0]], axis=1)
    enc = to_cells(encoder_inputs[0, 0])
    far_left = beside(enc[CELLS - 2 * Z :], 2)
    far_right = beside(enc[: 2 * Z], -2)
    left = beside(enc, 1)
    right = beside(enc, -1)
    rest = jnp.concatenate([to_cells(upper_inputs[0, 0]), to_cells(output_cotangent[0])], axis=0)
    rest_left = beside(rest, 1)
    rest_right = beside(rest, -1)
    enc_v, enc_h, enc_s1, enc_s2, enc_out = forward(
        encode_kernel, [sds(12, BF)],
        place, kernels, bias_rows, far_left, left, enc, right, far_right,
    )
    dec_v, dec_h, dec_s1, dec_s2 = forward(
        decode_kernel, [],
        place, kernels, bias_rows, enc_out, rest_left, rest, rest_right,
    )
    cot = (
        rest_left[2 * CELLS - 2 * Z :],
        rest[CELLS:],
        rest_right[CELLS : CELLS + 2 * Z],
    )
    slopes = (dec_s1, dec_s2)
    state = tick(2, None, place, kernels, slopes, cot)
    for turn in range(1, SECTIONS):
        cot = hand_on(state, turn - 1, 1)
        state = tick(2, turn, place, kernels, slopes, cot, state=state)
    upper = state
    skip = (beside(upper[4], 1), upper[2], beside(upper[3], -1))
    slopes = (enc_s1, enc_s2)
    state = tick(0, None, place, kernels, slopes, skip)
    for turn in range(SECTIONS - 2, -1, -1):
        cot = hand_on(state, turn + 1, -1)
        if turn == 1:
            dec_total = first_phases(place, (upper[1], dec_v, upper[0], dec_h))
        if turn > 0:
            state = tick(0, turn, place, kernels, slopes, cot, skip=skip, state=state)
    second, first, wide = final_tick(place, kernels, slopes, cot, skip, state)
    enc_total = first_phases(place, (first, enc_v, second, enc_h))
    last_grad = late_input_grad(place, kernels, wide, state[2])
    encoder_grad, upper_grad = from_cells(last_grad), from_cells(upper[2])
    mine = last_phases(place, [enc_total, dec_total])
    other = [send(part, core_step, 1) for part in mine]
    totals = unpack(place, 0, mine)
    weight_total, bias_total = unpack(place, 1, other, totals)
    return (
        encoder_grad,
        upper_grad,
        weight_total[None],
        bias_total.reshape(1, 4, C),
    )


def solution(mesh):
    return jax.shard_map(
        whole_pass,
        mesh=mesh,
        in_specs=(
            P("section", None, None, "space", None, None),
            P("section", None, None, "space", None, None),
            P(None, None, "space", None, None),
            P("section", None, None, None, None),
            P("section", None, None),
        ),
        out_specs=(
            P("section", None, None, "space", None, None),
            P("section", None, None, "space", None, None),
            P("section", None, None, None, None),
            P("section", None, None),
        ),
        check_vma=False,
    )
```
